32 devices in a mesh: slab: 2 (over x), row: 8 (over z, y), col: 2 (over core).
Axes of the slice: x: 2, y: 2, z: 4, core: 2. Of those that a mesh axis runs over, the one named last changes fastest.
Arguments:
- points: bfloat16 [9, 32, 131072], P(None, None, ('slab', 'row', 'col')), parts along dimension 2, may hold values from -6 to 6
- pillar_cell: int32 [131072], P(('slab', 'row', 'col')), parts along dimension 0, may hold values from 0 to 65535, as said below
- point_count: int32 [131072], P(('slab', 'row', 'col')), parts along dimension 0, may hold values from 1 to 32
- tile_count: int32 [512], P(('slab', 'row', 'col')), parts along dimension 0, may hold values from 0 to 256, as said below
- point_embed: bfloat16 [64, 9], replicated, may hold values from -3 to 3
- point_mix: bfloat16 [64, 64], replicated, may hold values from -1 to 1
- first_conv: bfloat16 [3, 3, 64, 64], replicated, may hold values from -0.375 to 0.375
- second_conv: bfloat16 [3, 3, 64, 64], replicated, may hold values from -0.375 to 0.375
- third_conv: bfloat16 [3, 3, 128, 64], replicated, may hold values from -0.375 to 0.375
- fourth_conv: bfloat16 [3, 3, 128, 128], replicated, may hold values from -0.25 to 0.25
- fifth_conv: bfloat16 [3, 3, 256, 128], replicated, may hold values from -0.25 to 0.25
- sixth_conv: bfloat16 [3, 3, 256, 256], replicated, may hold values from -0.1875 to 0.1875
- near_lift: bfloat16 [1, 1, 128, 64], replicated, may hold values from -1 to 1
- mid_lift: bfloat16 [2, 2, 128, 128], replicated, may hold values from -0.75 to 0.75
- far_lift: bfloat16 [4, 4, 128, 256], replicated, may hold values from -0.5 to 0.5
- biases: float32 [1408], replicated, may hold values from -1.5 to 1.5
Outputs:
- joined: bfloat16 [384, 256, 512], P(None, ('slab', 'row'), 'col'), parts along dimension 1
The draws below stay inside these ranges and needn't reach their ends.
There are 2 independent parts, one for each index of `slab`. The reference program is written for one: setup_inputs(seed, part) draws one part's arguments, and reference() takes and returns one part's arrays. A program takes and returns all parts, laid end to end along the dimension named above; an argument that names none is the same for every part. Nothing has to cross between parts.
Inputs may be any that keep to these rules, and one draw needn't show every extreme that they name: `tile_count`: entry s * 16 + t counts the live slots that device s (row-major over row and col) holds for tile t (row-major over row and col); they are the first of that tile's group of 256 slots. In every draw some tile gets exactly 256 live slots from every device. `pillar_cell`: slot s holds cell r * 512 + c; every slot in a device's group for tile t lies in tile t, whose rows and columns are those of device t; a cell may appear in several slots, on one device or several. `point_count`: the valid points of a slot are its first ones.
All inputs are finite; a program needn't handle non-finite values.
Results may differ from the reference program's by a relative error of at most 0.0081.
Values may be sent and summed in bfloat16 or wider, within the bound.
A program may use at most 64 MiB of HBM per device.

```python
import jax
import jax.numpy as jnp
from jax import lax

FEAT = 9
PTS = 32
PF = 64
C1 = 64
C2 = 128
C3 = 256
UP = 128
ROWS_DEV = 16
COLS_DEV = 256
CAP = 256
TILES = 16
ALLSLOTS = 65536
NROWS = 128
NCOLS = 512
BIAS_LEN = 1408


def draw_pillar_cell(key, part):
    col_tiles = NCOLS // COLS_DEV
    slot_index = jnp.arange(ALLSLOTS, dtype=jnp.int32)
    dest_tile = slot_index // CAP % TILES
    tile_row = dest_tile // col_tiles
    tile_col = dest_tile % col_tiles
    key_row, key_col = jax.random.split(jax.random.fold_in(key, 11))
    row_inside = jax.random.randint(key_row, (ALLSLOTS,), 0, ROWS_DEV, dtype=jnp.int32)
    col_inside = jax.random.randint(key_col, (ALLSLOTS,), 0, COLS_DEV, dtype=jnp.int32)
    return ((tile_row * ROWS_DEV + row_inside) * NCOLS + tile_col * COLS_DEV + col_inside).astype(jnp.int32)


def draw_tile_count(key, part):
    key_hot, key_load = jax.random.split(jax.random.fold_in(key, 23))
    hottest = jax.random.randint(key_hot, (), 0, TILES, dtype=jnp.int32)
    load_draw = jax.random.randint(key_load, (TILES, TILES), 0, CAP * 4 // 5 + 1, dtype=jnp.int32)
    dest_tile = lax.broadcasted_iota(jnp.int32, (TILES, TILES), 1)
    return jnp.where(dest_tile == hottest, CAP, load_draw).reshape(TILES * TILES).astype(jnp.int32)


def with_ends(values, rng, smallest, top_value):
    place = [jax.random.randint(jax.random.fold_in(rng, axis), (), 0, length) for axis, length in enumerate(values.shape)]
    widest = values.shape.index(max(values.shape))
    neighbour = place[:widest] + [(place[widest] + 1) % values.shape[widest]] + place[widest + 1:]
    return values.at[tuple(place)].set(smallest).at[tuple(neighbour)].set(top_value)


def steps_of(stream_key, dims, cuts, least, largest):
    loudness, own = 1.0, jax.random.fold_in(stream_key, 6)
    for axis_at, blocks in cuts:
        steps = jnp.exp(jax.random.uniform(jax.random.fold_in(own, axis_at), (blocks,), jnp.float32, least / len(cuts), largest / len(cuts)))
        loudness = loudness * jnp.repeat(steps, dims[axis_at] // blocks).reshape([-1 if axis == axis_at else 1 for axis in range(len(dims))])
    return loudness


def bell_draw(rng, shape, spread, most, shards=(), kind=jnp.bfloat16):
    drawn = spread * jax.random.normal(rng, shape, jnp.float32)
    if shards:
        drawn = drawn * steps_of(rng, shape, shards, -0.22, 0.18)
    return jnp.clip(drawn, -most, most).astype(kind)


def setup_inputs(seed: int = 0, part: int = 0) -> dict:
    keys = jax.random.split(jax.random.key(seed), 17)
    part_splits = jax.random.split(jax.random.fold_in(keys[16], part), 17)
    return {
        "points": bell_draw(part_splits[0], (FEAT, PTS, ALLSLOTS), 1.0, 6.0, ((2, 16),)),
        "pillar_cell": draw_pillar_cell(jax.random.fold_in(jax.random.fold_in(keys[16], part), 71), part),
        "point_count": with_ends(jax.random.randint(part_splits[2], (ALLSLOTS,), 1, PTS + 1), jax.random.fold_in(part_splits[2], 1), 1, PTS).astype(jnp.int32),
        "tile_count": draw_tile_count(jax.random.fold_in(jax.random.fold_in(keys[16], part), 71), part),
        "point_embed": bell_draw(keys[4], (PF, FEAT), (FEAT // 2) ** -0.5, 3.0),
        "point_mix": bell_draw(keys[5], (PF, PF), (PF // 2) ** -0.5, 1.0),
        "first_conv": bell_draw(keys[6], (3, 3, C1, PF), (9 * PF // 2) ** -0.5, 0.375),
        "second_conv": bell_draw(keys[7], (3, 3, C1, C1), (9 * C1 // 2) ** -0.5, 0.375),
        "third_conv": bell_draw(keys[8], (3, 3, C2, C1), (9 * C1 // 2) ** -0.5, 0.375),
        "fourth_conv": bell_draw(keys[9], (3, 3, C2, C2), (9 * C2 // 2) ** -0.5, 0.25),
        "fifth_conv": bell_draw(keys[10], (3, 3, C3, C2), (9 * C2 // 2) ** -0.5, 0.25),
        "sixth_conv": bell_draw(keys[11], (3, 3, C3, C3), (9 * C3 // 2) ** -0.5, 0.1875),
        "near_lift": bell_draw(keys[12], (1, 1, UP, C1), (C1 // 2) ** -0.5, 1.0),
        "mid_lift": bell_draw(keys[13], (2, 2, UP, C2), (C2 // 2) ** -0.5, 0.75),
        "far_lift": bell_draw(keys[14], (4, 4, UP, C3), (C3 // 2) ** -0.5, 0.5),
        "biases": bell_draw(keys[15], (BIAS_LEN,), 0.3, 1.5, (), jnp.float32),
    }


def encode_block(point_block, count_row, point_embed, point_mix, b_embed, b_mix):
    feat_in, point_num, slot_num = point_block.shape
    flat_rows = point_block.reshape(feat_in, point_num * slot_num)
    hidden = jnp.dot(point_embed, flat_rows, preferred_element_type=jnp.float32) + b_embed[:, None]
    hidden = jax.nn.relu(hidden).astype(jnp.bfloat16)
    second = jnp.dot(point_mix, hidden, preferred_element_type=jnp.float32) + b_mix[:, None]
    second = jax.nn.relu(second).reshape(-1, point_num, slot_num)
    valid_mask = lax.broadcasted_iota(jnp.int32, (point_num, slot_num), 0) < count_row[None, :]
    return jnp.max(jnp.where(valid_mask[None], second, 0.0), axis=1).astype(jnp.bfloat16)


def conv_layer(inputs, kernel, bias_vec, stride):
    summed = lax.conv_general_dilated(inputs[None], kernel, (stride, stride), ((1, 1), (1, 1)),
                                      dimension_numbers=("NCHW", "HWOI", "NCHW"),
                                      preferred_element_type=jnp.float32)[0]
    return jax.nn.relu(summed + bias_vec[:, None, None]).astype(jnp.bfloat16)


def lift_layer(inputs, kernel, bias_vec):
    factor = kernel.shape[0]
    product = jnp.einsum("abop,pij->oiajb", kernel.astype(jnp.float32), inputs.astype(jnp.float32))
    out_chan = kernel.shape[2]
    product = product.reshape(out_chan, inputs.shape[1] * factor, inputs.shape[2] * factor)
    return jax.nn.relu(product + bias_vec[:, None, None]).astype(jnp.bfloat16)


def reference(points, pillar_cell, point_count, tile_count, point_embed, point_mix, first_conv, second_conv,
              third_conv, fourth_conv, fifth_conv, sixth_conv, near_lift, mid_lift, far_lift, biases):
    extents = [PF, PF, C1, C1, C2, C2, C3, C3, UP, UP, UP]
    pieces = []
    offset = 0
    for extent in extents:
        pieces.append(biases[offset:offset + extent])
        offset += extent
    slot_index = jnp.arange(ALLSLOTS, dtype=jnp.int32)
    live_slot = (slot_index % CAP) < tile_count[slot_index // CAP]
    slot_points = jnp.where(live_slot, point_count, 0).astype(jnp.int32)

    def one_block(block_id):
        start = (block_id * CAP).astype(jnp.int32)
        point_block = lax.dynamic_slice_in_dim(points, start, CAP, 2)
        count_row = lax.dynamic_slice_in_dim(slot_points, start, CAP, 0)
        return encode_block(point_block, count_row, point_embed, point_mix, pieces[0], pieces[1])

    vectors = lax.map(one_block, jnp.arange(ALLSLOTS // CAP, dtype=jnp.int32))
    vectors = jnp.transpose(vectors, (1, 0, 2)).reshape(PF, ALLSLOTS)
    bev = jnp.zeros((PF, NROWS * NCOLS), jnp.bfloat16).at[:, pillar_cell].max(vectors)
    bev = bev.reshape(PF, NROWS, NCOLS)
    level_one = conv_layer(conv_layer(bev, first_conv, pieces[2], 1), second_conv, pieces[3], 1)
    level_two = conv_layer(conv_layer(level_one, third_conv, pieces[4], 2), fourth_conv, pieces[5], 1)
    level_three = conv_layer(conv_layer(level_two, fifth_conv, pieces[6], 2), sixth_conv, pieces[7], 1)
    near = lift_layer(level_one, near_lift, pieces[8])
    middle = lift_layer(level_two, mid_lift, pieces[9])
    distant = lift_layer(level_three, far_lift, pieces[10])
    return jnp.concatenate([near, middle, distant], axis=0)
```

```python
import jax
import jax.numpy as jnp
from jax import lax
from jax.experimental import pallas as pl
from jax.experimental.pallas import tpu as pltpu
from jax.sharding import PartitionSpec as P

ROWS_DEV = 16
COLS_DEV = 256
PACK = 4
HALF = 16
LANES = 4
SIDE = 16
TILE = 128


def encode_kernel(
    x_ref, count_ref, cell_ref, embed_ref, mix_ref, bias_ref, live_ref, out_ref, place_ref,
    send_ref, place_send, w1_ref, w2_ref, b1_ref, b2_ref, ssem, rsem, place_ssem, place_rsem
):
    feat, points, _ = x_ref.shape
    tiles, _, cap = count_ref.shape
    chan, mid = mix_ref.shape
    half = tiles // 2
    col_count = lax.axis_size("col")
    me = lax.axis_index("row") * col_count + lax.axis_index("col")

    def device_of(tile):
        return {"row": tile // col_count, "col": tile % col_count}

    barrier = pltpu.get_barrier_semaphore()

    def greet(i, carry):
        pl.semaphore_signal(
            barrier,
            inc=1,
            device_id=device_of((me + i) % tiles),
            device_id_type=pl.DeviceIdType.MESH,
        )
        return carry

    lax.fori_loop(1, tiles, greet, 0)

    wide = feat * HALF
    lane = lax.broadcasted_iota(jnp.int32, (feat, wide), 1)
    spread = lane // HALF == lax.broadcasted_iota(jnp.int32, (feat, wide), 0)
    spread = jnp.where(spread, 1.0, 0.0).astype(jnp.bfloat16)
    full = lax.dot_general(
        embed_ref[...], spread, (((0,), (0,)), ((), ())), preferred_element_type=jnp.float32
    )
    point = lax.broadcasted_iota(jnp.int32, (mid, wide), 1) % HALF
    for q in range(HALF // PACK):
        for p in range(PACK):
            part = jnp.where(point == q * PACK + p, full, 0.0)
            w1_ref[q, p * mid : (p + 1) * mid, :] = part.astype(jnp.bfloat16)
    w2_ref[...] = jnp.zeros_like(w2_ref)
    for p in range(PACK):
        w2_ref[p * chan : (p + 1) * chan, p * mid : (p + 1) * mid] = mix_ref[...]
    both = mid + chan
    column = jnp.broadcast_to(bias_ref[0:1, :], (both, both)).T[:, 0:1]
    for p in range(PACK):
        b1_ref[p * mid : (p + 1) * mid, :] = column[0:mid]
    b2_ref[...] = column[mid:both]
    cell = cell_ref[...]
    row = cell // (COLS_DEV * col_count) % ROWS_DEV
    place_send[...] = row * COLS_DEV + cell % COLS_DEV

    def encode(tile, dest_ref):
        slot = lax.broadcasted_iota(jnp.int32, (1, cap), 1)
        count = jnp.where(slot < live_ref[tile], count_ref[tile], 0)
        start = pl.multiple_of(tile * cap, cap)
        best = jnp.full((chan, cap), -jnp.inf, jnp.float32)
        for h in range(points // HALF):
            block = x_ref[:, h * HALF : (h + 1) * HALF, pl.ds(start, cap)]
            block = block.reshape(feat * HALF, cap)
            for q in range(HALF // PACK):
                hidden = jnp.dot(w1_ref[q], block, preferred_element_type=jnp.float32)
                hidden = jnp.maximum(hidden + b1_ref[...], 0.0).astype(jnp.bfloat16)
                second = jnp.dot(w2_ref[...], hidden, preferred_element_type=jnp.float32)
                for p in range(PACK):
                    j = h * HALF + q * PACK + p
                    part = second[p * chan : (p + 1) * chan]
                    best = jnp.maximum(best, jnp.where(count > j, part, -jnp.inf))
        vec = jnp.maximum(best + b2_ref[...], 0.0)
        dest_ref[tile] = vec.astype(jnp.bfloat16)

    def place_of(i, slot):
        tile = (me + i) % tiles
        return pltpu.make_async_remote_copy(
            src_ref=place_send.at[tile],
            dst_ref=place_ref.at[slot],
            send_sem=place_ssem.at[i],
            recv_sem=place_rsem.at[i],
            device_id=device_of(tile),
            device_id_type=pl.DeviceIdType.MESH,
        )

    def copy_of(i, slot):
        tile = (me + i) % tiles
        return pltpu.make_async_remote_copy(
            src_ref=send_ref.at[tile],
            dst_ref=out_ref.at[slot],
            send_sem=ssem.at[i],
            recv_sem=rsem.at[i],
            device_id=device_of(tile),
            device_id_type=pl.DeviceIdType.MESH,
        )

    pl.semaphore_wait(barrier, tiles - 1)

    def step(k, carry):
        i = half + (1 - 2 * (k % 2)) * ((k + 1) // 2)
        encode((me + i) % tiles, send_ref)
        copy_of(i, me).start()
        place_of(i, me).start()
        return carry

    lax.fori_loop(0, tiles - 1, step, 0, unroll=3)
    encode(me, out_ref)
    place_ref[me] = place_send[me]

    def finish(i, carry):
        copy_of(i, me).wait_send()
        place_of(i, me).wait_send()
        copy_of(i, (me - i + tiles) % tiles).wait_recv()
        place_of(i, (me - i + tiles) % tiles).wait_recv()
        return carry

    lax.fori_loop(1, tiles, finish, 0)


def encode_all(points, counts, cells, live, embed, mix, bias):
    feat = points.shape[0]
    tiles, _, cap = counts.shape
    chan, mid = mix.shape
    vmem = pl.BlockSpec(memory_space=pltpu.VMEM)
    return pl.pallas_call(
        encode_kernel,
        in_specs=[vmem] * 6 + [pl.BlockSpec(memory_space=pltpu.SMEM)],
        out_specs=[vmem, vmem],
        out_shape=[
            jax.ShapeDtypeStruct((tiles, chan, cap), jnp.bfloat16),
            jax.ShapeDtypeStruct((tiles, 1, cap), jnp.int32),
        ],
        scratch_shapes=[
            pltpu.VMEM((tiles, chan, cap), jnp.bfloat16),
            pltpu.VMEM((tiles, 1, cap), jnp.int32),
            pltpu.VMEM((HALF // PACK, PACK * mid, feat * HALF), jnp.bfloat16),
            pltpu.VMEM((PACK * chan, PACK * mid), jnp.bfloat16),
            pltpu.VMEM((PACK * mid, 1), jnp.float32),
            pltpu.VMEM((chan, 1), jnp.float32),
            pltpu.SemaphoreType.DMA((tiles,)),
            pltpu.SemaphoreType.DMA((tiles,)),
            pltpu.SemaphoreType.DMA((tiles,)),
            pltpu.SemaphoreType.DMA((tiles,)),
        ],
        compiler_params=pltpu.CompilerParams(collective_id=7, has_side_effects=True),
        name="encode_send",
    )(points, counts, cells, embed, mix, bias, live)


def scatter_kernel(cell_ref, vec_ref, out_ref, stage, *grids):
    tiles, chan, cap = vec_ref.shape
    area = out_ref.shape[0]
    for grid in grids:
        grid[...] = jnp.zeros_like(grid)
    lanes = len(grids)
    first_half = lax.broadcasted_iota(jnp.int32, (cap, 2 * chan), 1) < chan

    def per_tile(t, carry):
        twice = vec_ref[t].astype(jnp.float32)
        twice = jnp.concatenate([twice, twice], axis=0).T
        stage[0:cap, :] = jnp.where(first_half, twice, 0.0)
        stage[cap : 2 * cap, :] = jnp.where(first_half, 0.0, twice)
        unroll = 32 // lanes

        def per_slot(s, inner):
            for k in range(unroll):
                base = (s * unroll + k) * lanes
                cells = [cell_ref[t * cap + base + a] for a in range(lanes)]
                pairs = [lax.shift_right_logical(cell, 1) for cell in cells]
                rows = [base + a + (cells[a] & 1) * cap for a in range(lanes)]
                olds = [grids[a][pl.ds(pairs[a], 1), :] for a in range(lanes)]
                for a in range(lanes):
                    grids[a][pl.ds(pairs[a], 1), :] = jnp.maximum(
                        olds[a], stage[pl.ds(rows[a], 1), :]
                    )
            return inner

        return lax.fori_loop(0, cap // (lanes * unroll), per_slot, carry)

    lax.fori_loop(0, tiles, per_tile, 0)
    total = grids[0][...]
    for grid in grids[1:]:
        total = jnp.maximum(total, grid[...])
    out_ref[...] = total.astype(jnp.bfloat16)


def scatter_max(cells, vectors):
    tiles, chan, cap = vectors.shape
    area = ROWS_DEV * COLS_DEV // 2
    return pl.pallas_call(
        scatter_kernel,
        in_specs=[
            pl.BlockSpec(memory_space=pltpu.SMEM),
            pl.BlockSpec(memory_space=pltpu.VMEM),
        ],
        out_specs=pl.BlockSpec(memory_space=pltpu.VMEM),
        out_shape=jax.ShapeDtypeStruct((area, 2 * chan), jnp.bfloat16),
        scratch_shapes=[pltpu.VMEM((2 * cap, 2 * chan), jnp.float32)]
        + [pltpu.VMEM((area, 2 * chan), jnp.float32)] * LANES,
        name="scatter_max",
    )(cells, vectors)


STEPS = [(dr, dc) for dr in (1, -1) for dc in (0, 1, -1)] + [(0, 1), (0, -1)]


class Halo:
    def __init__(self, stage, own, top, bottom, left, right, send_sem, recv_sem):
        self.stage, self.own = stage, own
        self.top, self.bottom, self.left, self.right = top, bottom, left, right
        self.send_sem, self.recv_sem = send_sem, recv_sem
        self.rows, self.width, _ = own.shape
        self.before, self.after = top.shape[0], bottom.shape[0]
        self.count_rows, self.count_cols = lax.axis_size("row"), lax.axis_size("col")
        self.my_row, self.my_col = lax.axis_index("row"), lax.axis_index("col")
        self.steps = [
            (dr, dc)
            for dr, dc in STEPS
            if (dr == 0 or self.count_rows > 1) and (dc == 0 or self.count_cols > 1)
        ]

    def exists(self, dr, dc):
        row, col = self.my_row + dr, self.my_col + dc
        return (row >= 0) & (row < self.count_rows) & (col >= 0) & (col < self.count_cols)

    def peer(self, dr, dc):
        return {"row": self.my_row + dr, "col": self.my_col + dc}

    def clear(self):
        for ref in (self.top, self.bottom, self.left, self.right):
            ref[...] = jnp.zeros_like(ref)

    def copy_of(self, place):
        dr, dc = self.steps[place]
        before, rows, after = self.before, self.rows, self.after
        row_from = {1: slice(rows - before, rows), 0: slice(0, rows), -1: slice(0, after)}[dr]
        col_from = {1: slice(self.width - SIDE, self.width), 0: slice(0, self.width), -1: slice(0, SIDE)}[dc]
        row_to = {
            1: slice(0, before),
            0: slice(before, before + rows),
            -1: slice(before + rows, before + rows + after),
        }[dr]
        if dc == 0:
            target = self.top if dr == 1 else self.bottom
        else:
            target = (self.left if dc == 1 else self.right).at[row_to]
        return pltpu.make_async_remote_copy(
            src_ref=self.own.at[row_from, col_from, :],
            dst_ref=target,
            send_sem=self.send_sem.at[self.stage, place],
            recv_sem=self.recv_sem.at[self.stage, place],
            device_id=self.peer(dr, dc),
            device_id_type=pl.DeviceIdType.MESH,
        )

    def each(self, keep, sign, action):
        for place, (dr, dc) in enumerate(self.steps):
            if keep(dr, dc):

                @pl.when(self.exists(sign * dr, sign * dc))
                def _():
                    action(self.copy_of(place))

    def start(self, keep):
        self.each(keep, 1, lambda copy: copy.start())

    def wait_send(self):
        self.each(lambda dr, dc: True, 1, lambda copy: copy.wait_send())

    def wait_recv(self, keep):
        self.each(keep, -1, lambda copy: copy.wait_recv())


def across(dr, dc):
    return dr != 0


def beside(dr, dc):
    return dr == 0


def levels_kernel(
    bev_ref, w1a_ref, w1b_ref, w2a_ref, w2b_ref, w3a_ref, w3b_ref, bias_ref,
    one_ref, two_ref, three_ref,
    top0, bottom0, left0, right0, top1, bottom1, left1, right1, top2, bottom2, left2, right2,
    send_sem, recv_sem,
    t1a, t1b, t2a, t2b, t3a, t3b, cat1a, cat1b, cat2e, cat2o, cat2b, cat3e, cat3o, cat3b,
    stage, stage3, stage4,
):
    rows1, pairs, _ = bev_ref.shape
    rows2, cols2, chan2 = two_ref.shape
    rows3, cols3, chan3 = three_ref.shape
    chan1 = w1a_ref.shape[2]
    mid1 = pairs + 16
    mid3 = cols3 + 16
    zero = Halo(0, bev_ref, top0, bottom0, left0, right0, send_sem, recv_sem)
    one = Halo(1, one_ref, top1, bottom1, left1, right1, send_sem, recv_sem)
    two = Halo(2, two_ref, top2, bottom2, left2, right2, send_sem, recv_sem)
    for halo in (zero, one, two):
        halo.clear()
    barrier = pltpu.get_barrier_semaphore()
    for dr, dc in zero.steps:

        @pl.when(zero.exists(dr, dc))
        def _():
            pl.semaphore_signal(
                barrier, inc=1, device_id=zero.peer(dr, dc), device_id_type=pl.DeviceIdType.MESH
            )

    def blocks(w_ref, u):
        wide = [w_ref[u, v].astype(jnp.float32) for v in range(3)]
        nil = jnp.zeros((chan1, chan1), jnp.float32)
        upper = jnp.concatenate([wide[1], wide[0]], axis=0)
        lower = jnp.concatenate([wide[2], wide[1]], axis=0)
        after = jnp.concatenate([nil, wide[2]], axis=0)
        prior = jnp.concatenate([wide[0], nil], axis=0)
        return jnp.concatenate([part.T for part in (upper, lower, after, prior)], axis=0)

    depth = 4 * chan1
    for w_ref, t_ref in ((w1a_ref, t1a), (w1b_ref, t1b)):
        for u in range(3):
            t_ref[u * depth : (u + 1) * depth, :] = blocks(w_ref, u).astype(jnp.bfloat16)

    peers = sum(jnp.where(zero.exists(dr, dc), 1, 0) for dr, dc in zero.steps)
    pl.semaphore_wait(barrier, peers)
    zero.start(lambda dr, dc: True)

    for u in range(3):
        base = u * depth
        t2a[base : base + chan1, :] = w2a_ref[u, 1]
        t2a[base + chan1 : base + 2 * chan1, :] = w2a_ref[u, 2]
        t2a[base + 2 * chan1 : base + 3 * chan1, :] = jnp.zeros((chan1, chan2), jnp.bfloat16)
        t2a[base + 3 * chan1 : base + 4 * chan1, :] = w2a_ref[u, 0]
    for w_ref, t_ref in ((w2b_ref, t2b), (w3a_ref, t3a), (w3b_ref, t3b)):
        deep = w_ref.shape[3]
        for u in range(3):
            for v in range(3):
                flip = w_ref[u, v].astype(jnp.float32).T
                t_ref[(3 * u + v) * deep : (3 * u + v + 1) * deep, :] = flip.astype(jnp.bfloat16)
    stage[...] = jnp.zeros_like(stage)
    stage3[...] = jnp.zeros_like(stage3)
    stage4[...] = jnp.zeros_like(stage4)

    half = lax.broadcasted_iota(jnp.int32, (mid1, TILE), 1) < chan1
    half_own = lax.broadcasted_iota(jnp.int32, (pairs, TILE), 1) < chan1
    has_left, has_right = zero.exists(0, -1), zero.exists(0, 1)
    has_up, has_down = zero.exists(-1, 0), zero.exists(1, 0)
    ways = stage.shape[0]

    def at(i, size):
        return pl.ds(pl.multiple_of(i * size, 16), size)

    def load(halo, r, own_row):
        left = halo.left[r].astype(jnp.float32)
        right = halo.right[r].astype(jnp.float32)
        return left, own_row.astype(jnp.float32), right

    def spread(halo, r, own_row, way):
        left, row, right = load(halo, r, own_row)
        center = jnp.concatenate([left[8:16], row, right[0:8]], axis=0)
        stage[way, 8 : 8 + mid1, :] = center
        return center

    def fill1a(r, own_row, way):
        center = spread(zero, r, own_row, way)
        near = jnp.where(half, stage[way, 9 : 9 + mid1, :], stage[way, 7 : 7 + mid1, :])
        cat1a[at(r, mid1), :] = jnp.concatenate([center, near], axis=1).astype(jnp.bfloat16)

    def fill2a(r, target, own_row, way):
        center = spread(one, r, own_row, way)
        cat_row = jnp.concatenate([center, stage[way, 7 : 7 + mid1, :]], axis=1)
        target[at(r // 2, mid1), :] = cat_row.astype(jnp.bfloat16)

    def fill3a(r, target, own_row, way):
        left, row, right = load(two, r, own_row)
        stage3[way, 8 : 8 + SIDE, :] = left
        stage3[way, 8 + SIDE : 8 + SIDE + cols2, :] = row
        stage3[way, 8 + SIDE + cols2 : 8 + 2 * SIDE + cols2, :] = right
        parts = [stage3[way, pl.ds(7 + v, mid3, stride=2), :] for v in range(3)]
        target[at(r // 2, mid3), :] = jnp.concatenate(parts, axis=1).astype(jnp.bfloat16)

    def bias_of(at_row, times, width):
        return bias_ref[at_row : at_row + 1, 0:width] if times == 1 else None

    bias1a = jnp.concatenate([bias_ref[1:2, 0:chan1]] * 2, axis=1)
    bias1b = jnp.concatenate([bias_ref[1:2, chan1 : 2 * chan1]] * 2, axis=1)
    bias2a, bias2b = bias_ref[2:3, :], bias_ref[3:4, :]
    bias3a = jnp.concatenate([bias_ref[4:5, :], bias_ref[5:6, :]], axis=1)
    bias3b = jnp.concatenate([bias_ref[6:7, :], bias_ref[7:8, :]], axis=1)

    def masked(row, row_good):
        first = jnp.where(has_left & row_good, row[0:8], 0.0)
        last = jnp.where(has_right & row_good, row[row.shape[0] - 8 :], 0.0)
        inner = row[8 : row.shape[0] - 8]
        if row_good is not True:
            inner = jnp.where(row_good, inner, 0.0)
        return jnp.concatenate([first, inner, last], axis=0)

    def conv(lhs, weight, bias):
        total = jnp.dot(jnp.concatenate(lhs, axis=1), weight[...], preferred_element_type=jnp.float32)
        return jnp.maximum(total + bias, 0.0)

    def mid_one(i, count, good):
        lhs = [cat1a[pl.ds(pl.multiple_of((i + u) * mid1, 16), count * mid1), :] for u in range(3)]
        total = conv(lhs, t1a, bias1a)
        for k in range(count):
            row = masked(total[k * mid1 : (k + 1) * mid1], good)
            stage[k, 8 : 8 + mid1, :] = row
            near = jnp.where(half_own, stage[k, 17 : 17 + pairs, :], stage[k, 15 : 15 + pairs, :])
            cat_row = jnp.concatenate([row[8 : 8 + pairs], near], axis=1)
            cat1b[at(i + k, pairs), :] = cat_row.astype(jnp.bfloat16)

    def out_one(i, count):
        lhs = [cat1b[pl.ds(pl.multiple_of((i + u) * pairs, 16), count * pairs), :] for u in range(3)]
        total = conv(lhs, t1b, bias1b).astype(jnp.bfloat16)
        for k in range(count):
            one_ref[i + k] = total[k * pairs : (k + 1) * pairs]

    def mid_two(i, count, good):
        even = [cat2e[pl.ds((i + d) * mid1, count * mid1), :] for d in range(2)]
        odd = cat2o[pl.ds(i * mid1, count * mid1), :]
        total = conv([even[0], odd, even[1]], t2a, bias2a)
        for k in range(count):
            row = masked(total[k * mid1 : (k + 1) * mid1], good)
            stage[k % ways, 8 : 8 + mid1, :] = row
            down = stage[k % ways, 15 : 15 + cols2, :]
            up = stage[k % ways, 17 : 17 + cols2, :]
            cat_row = jnp.concatenate([down, row[8 : 8 + cols2], up], axis=1)
            cat2b[at(i + k, cols2), :] = cat_row.astype(jnp.bfloat16)

    def out_two(i, count):
        lhs = [cat2b[pl.ds((i + u) * cols2, count * cols2), :] for u in range(3)]
        total = conv(lhs, t2b, bias2b).astype(jnp.bfloat16)
        for k in range(count):
            two_ref[i + k] = total[k * cols2 : (k + 1) * cols2]

    def mid_three(i, count, good):
        even = [cat3e[pl.ds((i + d) * mid3, count * mid3), :] for d in range(2)]
        odd = cat3o[pl.ds(i * mid3, count * mid3), :]
        total = conv([even[0], odd, even[1]], t3a, bias3a)
        for k in range(count):
            row = masked(total[k * mid3 : (k + 1) * mid3], good)
            stage4[k % ways, 8 : 8 + mid3, :] = row
            down = stage4[k % ways, 15 : 15 + cols3, :]
            up = stage4[k % ways, 17 : 17 + cols3, :]
            cat_row = jnp.concatenate([down, row[8 : 8 + cols3], up], axis=1)
            cat3b[at(i + k, cols3), :] = cat_row.astype(jnp.bfloat16)

    zero.wait_recv(beside)

    def inner_fill(g, carry):
        for k in range(4):
            r = g * 4 + k
            fill1a(r + 2, bev_ref[r], k)
        return carry

    lax.fori_loop(0, rows1 // 4, inner_fill, 0)

    def inner_mid(g, carry):
        mid_one(2 + g * 2, 2, True)
        return carry

    lax.fori_loop(0, (rows1 - 2) // 2, inner_mid, 0)

    def inner_out(g, carry):
        out_one(2 + g * 2, 2)
        return carry

    lax.fori_loop(0, (rows1 - 4) // 2, inner_out, 0)
    zero.wait_recv(across)
    for k in range(2):
        fill1a(k, top0[k], k)
        fill1a(rows1 + 2 + k, bottom0[k], 2 + k)
    mid_one(0, 1, has_up)
    mid_one(1, 1, True)
    mid_one(rows1, 1, True)
    mid_one(rows1 + 1, 1, has_down)
    out_one(0, 2)
    out_one(rows1 - 2, 2)
    one.start(lambda dr, dc: True)

    one.wait_recv(beside)

    def inner_fill2(g, carry):
        for k in range(2):
            r = g * 4 + 2 * k
            fill2a(r + 3, cat2o, one_ref[r], 2 * k)
            fill2a(r + 4, cat2e, one_ref[r + 1], 2 * k + 1)
        return carry

    lax.fori_loop(0, rows1 // 4, inner_fill2, 0)
    for i in range(2, rows2, 2):
        mid_two(i, 2, True)
    mid_two(rows2, 1, True)
    for i in range(2, rows2 - 2, 2):
        out_two(i, 2)
    out_two(rows2 - 2, 1)
    one.wait_recv(across)
    fill2a(0, cat2e, top1[0], 0)
    fill2a(1, cat2o, top1[1], 1)
    fill2a(2, cat2e, top1[2], 2)
    fill2a(rows1 + 3, cat2o, bottom1[0], 3)
    fill2a(rows1 + 4, cat2e, bottom1[1], 0)
    mid_two(0, 1, has_up)
    mid_two(1, 1, True)
    mid_two(rows2 + 1, 1, has_down)
    out_two(0, 2)
    out_two(rows2 - 1, 1)
    two.start(lambda dr, dc: True)

    two.wait_recv(beside)
    for r in range(rows2):
        fill3a(r + 3, cat3o if r % 2 == 0 else cat3e, two_ref[r], r % ways)
    mid_three(2, rows3 - 1, True)
    two.wait_recv(across)
    fill3a(0, cat3e, top2[0], 0)
    fill3a(1, cat3o, top2[1], 1)
    fill3a(2, cat3e, top2[2], 2)
    fill3a(rows2 + 3, cat3o, bottom2[0], 3)
    fill3a(rows2 + 4, cat3e, bottom2[1], 0)
    mid_three(0, 1, has_up)
    mid_three(1, 1, True)
    mid_three(rows3 + 1, 1, has_down)
    lhs = [cat3b[u * cols3 : (u + rows3) * cols3, :] for u in range(3)]
    total = conv(lhs, t3b, bias3b).astype(jnp.bfloat16)
    three_ref[...] = total.reshape(rows3, cols3, chan3)
    for halo in (zero, one, two):
        halo.wait_send()


def levels(bev, convs, bias):
    rows1, pairs, _ = bev.shape
    w1a, w1b, w2a, w2b, w3a, w3b = convs
    chan1, chan2, chan3 = w1a.shape[2], w2b.shape[2], w3b.shape[2]
    rows2, rows3, cols2, cols3 = rows1 // 2, rows1 // 4, pairs, pairs // 2
    vmem = pl.BlockSpec(memory_space=pltpu.VMEM)
    mid1, mid3 = pairs + 16, cols3 + 16

    def buffers(rows, before, after):
        return [
            pltpu.VMEM((before, pairs, TILE), jnp.bfloat16),
            pltpu.VMEM((after, pairs, TILE), jnp.bfloat16),
            pltpu.VMEM((before + rows + after, SIDE, TILE), jnp.bfloat16),
            pltpu.VMEM((before + rows + after, SIDE, TILE), jnp.bfloat16),
        ]

    def half(*shape):
        return pltpu.VMEM(shape, jnp.bfloat16)

    return pl.pallas_call(
        levels_kernel,
        in_specs=[vmem] * 8,
        out_specs=[vmem] * 3,
        out_shape=[
            jax.ShapeDtypeStruct((rows1, pairs, TILE), jnp.bfloat16),
            jax.ShapeDtypeStruct((rows2, cols2, chan2), jnp.bfloat16),
            jax.ShapeDtypeStruct((rows3, cols3, chan3), jnp.bfloat16),
        ],
        scratch_shapes=buffers(rows1, 2, 2)
        + buffers(rows1, 3, 2)
        + buffers(rows2, 3, 2)
        + [pltpu.SemaphoreType.DMA((3, len(STEPS)))] * 2
        + [
            half(12 * chan1, 2 * chan1),
            half(12 * chan1, 2 * chan1),
            half(12 * chan1, chan2),
            half(9 * chan2, chan2),
            half(9 * chan2, chan3),
            half(9 * chan3, chan3),
            half((rows1 + 4) * mid1, 4 * chan1),
            half((rows1 + 2) * pairs, 4 * chan1),
            half((rows2 + 3) * mid1, 4 * chan1),
            half((rows2 + 2) * mid1, 4 * chan1),
            half((rows2 + 2) * cols2, 3 * chan2),
            half((rows3 + 3) * mid3, 3 * chan2),
            half((rows3 + 2) * mid3, 3 * chan2),
            half((rows3 + 2) * cols3, 3 * chan3),
            pltpu.VMEM((4, mid1 + 16, TILE), jnp.float32),
            pltpu.VMEM((4, cols2 + 2 * SIDE + 16, TILE), jnp.float32),
            pltpu.VMEM((4, mid3 + 16, chan3), jnp.float32),
        ],
        compiler_params=pltpu.CompilerParams(collective_id=8, has_side_effects=True),
        name="levels",
    )(bev, *convs, bias)


def lift_kernel(
    one_ref, two_ref, three_ref, near_ref, mid_ref, far_ref, bias_ref, out_ref,
    result, expand1, expand2, expand3, gather, sem,
):
    rows, pairs, _ = one_ref.shape
    up = near_ref.shape[1]
    cols = 2 * pairs
    near = near_ref[...].astype(jnp.float32)
    near = jnp.concatenate([near, near], axis=0).T.astype(jnp.bfloat16)
    expand2[...] = jnp.zeros_like(expand2)
    expand3[...] = jnp.zeros_like(expand3)
    first_half = lax.broadcasted_iota(jnp.int32, (pairs, TILE), 1) < TILE // 2

    def product(weight, wide):
        return lax.dot_general(
            weight, wide, (((1,), (1,)), ((), ())), preferred_element_type=jnp.float32
        )

    def put(row, value, bias):
        for h in range(cols // TILE):
            piece = jnp.maximum(value[:, h * TILE : (h + 1) * TILE] + bias, 0.0)
            gather[h, pl.ds(row, up, stride=rows), :] = piece

    def finish(which):
        for h in range(cols // TILE):
            done = gather[h].astype(jnp.bfloat16).reshape(up, rows, TILE)
            result[which, :, :, h * TILE : (h + 1) * TILE] = done
        pltpu.make_async_copy(
            result.at[which], out_ref.at[pl.ds(which * up, up)], sem.at[which]
        ).start()

    def bias_tile(at_row):
        return jnp.broadcast_to(bias_ref[at_row : at_row + 1, :], (TILE, up)).T

    bias = bias_tile(8)
    for r in range(rows):
        row = one_ref[r].astype(jnp.float32)
        way = r % 2
        expand1[way, pl.ds(0, pairs, stride=2), :] = jnp.where(first_half, row, 0.0)
        expand1[way, pl.ds(1, pairs, stride=2), :] = jnp.where(first_half, 0.0, row)
        put(r, product(near, expand1[way].astype(jnp.bfloat16)), bias)
    finish(0)

    bias = bias_tile(9)
    factor = mid_ref.shape[0]
    weight = [
        jnp.concatenate([mid_ref[a, e] for e in range(factor)], axis=1) for a in range(factor)
    ]
    weight = jnp.concatenate(weight, axis=0)
    for i in range(two_ref.shape[0]):
        row = two_ref[i].astype(jnp.float32)
        way = i % 2
        for e in range(factor):
            expand2[way, e, pl.ds(e, row.shape[0], stride=factor), :] = row
        wide = jnp.concatenate([expand2[way, e] for e in range(factor)], axis=1)
        total = product(weight, wide.astype(jnp.bfloat16))
        for a in range(factor):
            put(i * factor + a, total[a * up : (a + 1) * up], bias)
    finish(1)

    bias = bias_tile(10)
    factor = far_ref.shape[0]
    weight = [
        jnp.concatenate([far_ref[a, e] for e in range(factor)], axis=1) for a in range(factor)
    ]
    weight = jnp.concatenate(weight, axis=0)
    halves = three_ref.shape[2] // TILE
    for i in range(three_ref.shape[0]):
        row = three_ref[i].astype(jnp.float32)
        for e in range(factor):
            for h in range(halves):
                expand3[e * halves + h, pl.ds(e, row.shape[0], stride=factor), :] = row[
                    :, h * TILE : (h + 1) * TILE
                ]
        wide = jnp.concatenate([expand3[k] for k in range(factor * halves)], axis=1)
        total = product(weight, wide.astype(jnp.bfloat16))
        for a in range(factor):
            put(i * factor + a, total[a * up : (a + 1) * up], bias)
    finish(2)
    for which in range(3):
        pltpu.make_async_copy(
            result.at[which], out_ref.at[pl.ds(which * up, up)], sem.at[which]
        ).wait()


def lifts(maps, weights, bias):
    rows, pairs, _ = maps[0].shape
    near, mid, far = weights
    up = near.shape[1]
    cols = 2 * pairs
    vmem = pl.BlockSpec(memory_space=pltpu.VMEM)
    factor, halves = far.shape[0], far.shape[3] // TILE
    return pl.pallas_call(
        lift_kernel,
        in_specs=[vmem] * 7,
        out_specs=pl.BlockSpec(memory_space=pl.ANY),
        out_shape=jax.ShapeDtypeStruct((3 * up, rows, cols), jnp.bfloat16),
        scratch_shapes=[
            pltpu.VMEM((3, up, rows, cols), jnp.bfloat16),
            pltpu.VMEM((2, cols, TILE), jnp.float32),
            pltpu.VMEM((2, mid.shape[0], cols, TILE), jnp.float32),
            pltpu.VMEM((factor * halves, cols, TILE), jnp.float32),
            pltpu.VMEM((cols // TILE, up * rows, TILE), jnp.float32),
            pltpu.SemaphoreType.DMA((3,)),
        ],
        name="lifts",
    )(*maps, near, mid, far, bias)


def on_device(
    points,
    pillar_cell,
    point_count,
    tile_count,
    point_embed,
    point_mix,
    first_conv,
    second_conv,
    third_conv,
    fourth_conv,
    fifth_conv,
    sixth_conv,
    near_lift,
    mid_lift,
    far_lift,
    biases,
):
    tile_num = tile_count.shape[0]
    capacity = points.shape[2] // tile_num
    bias = biases.reshape(-1, TILE)
    vectors, places = encode_all(
        points,
        point_count.reshape(tile_num, 1, capacity),
        pillar_cell.reshape(tile_num, 1, capacity),
        tile_count,
        jnp.transpose(point_embed),
        point_mix,
        bias,
    )
    chan = point_mix.shape[0]
    bev = scatter_max(places.reshape(-1), vectors)
    bev = bev.reshape(ROWS_DEV, COLS_DEV // 2, 2 * chan)
    convs = (
        first_conv,
        second_conv,
        jnp.transpose(third_conv, (0, 1, 3, 2)),
        fourth_conv,
        fifth_conv,
        sixth_conv,
    )
    maps = levels(bev, convs, bias)
    near = jnp.transpose(near_lift, (0, 1, 3, 2)).reshape(near_lift.shape[3], near_lift.shape[2])
    return lifts(maps, (near, mid_lift, far_lift), bias)


def solution(mesh):
    return jax.shard_map(
        on_device,
        mesh=mesh,
        in_specs=(
            P(None, None, ("slab", "row", "col")),
            P(("slab", "row", "col")),
            P(("slab", "row", "col")),
            P(("slab", "row", "col")),
            P(),
            P(),
            P(),
            P(),
            P(),
            P(),
            P(),
            P(),
            P(),
            P(),
            P(),
            P(),
        ),
        out_specs=P(None, ("slab", "row"), "col"),
        check_vma=False,
    )
```

```python
import jax
import jax.numpy as jnp
from jax import lax
from jax.experimental import pallas as pl
from jax.experimental.pallas import tpu as pltpu
from jax.sharding import PartitionSpec as P

ROWS_DEV = 16
COLS_DEV = 256
PACK = 4
HALF = 16
LANES = 4
SIDE = 16
TILE = 128


def encode_kernel(
    x_ref, count_ref, cell_ref, embed_ref, mix_ref, bias_ref, live_ref, out_ref, place_ref,
    send_ref, place_send, w1_ref, w2_ref, b1_ref, b2_ref, ssem, rsem, place_ssem, place_rsem
):
    feat, points, _ = x_ref.shape
    tiles, _, cap = count_ref.shape
    chan, mid = mix_ref.shape
    half = tiles // 2
    col_count = lax.axis_size("col")
    me = lax.axis_index("row") * col_count + lax.axis_index("col")

    def device_of(tile):
        return {"row": tile // col_count, "col": tile % col_count}

    barrier = pltpu.get_barrier_semaphore()

    def greet(i, carry):
        pl.semaphore_signal(
            barrier,
            inc=1,
            device_id=device_of((me + i) % tiles),
            device_id_type=pl.DeviceIdType.MESH,
        )
        return carry

    lax.fori_loop(1, tiles, greet, 0)

    wide = feat * HALF
    lane = lax.broadcasted_iota(jnp.int32, (feat, wide), 1)
    spread = lane // HALF == lax.broadcasted_iota(jnp.int32, (feat, wide), 0)
    spread = jnp.where(spread, 1.0, 0.0).astype(jnp.bfloat16)
    full = lax.dot_general(
        embed_ref[...], spread, (((0,), (0,)), ((), ())), preferred_element_type=jnp.float32
    )
    point = lax.broadcasted_iota(jnp.int32, (mid, wide), 1) % HALF
    for q in range(HALF // PACK):
        for p in range(PACK):
            part = jnp.where(point == q * PACK + p, full, 0.0)
            w1_ref[q, p * mid : (p + 1) * mid, :] = part.astype(jnp.bfloat16)
    w2_ref[...] = jnp.zeros_like(w2_ref)
    for p in range(PACK):
        w2_ref[p * chan : (p + 1) * chan, p * mid : (p + 1) * mid] = mix_ref[...]
    both = mid + chan
    column = jnp.broadcast_to(bias_ref[0:1, :], (both, both)).T[:, 0:1]
    for p in range(PACK):
        b1_ref[p * mid : (p + 1) * mid, :] = column[0:mid]
    b2_ref[...] = column[mid:both]
    cell = cell_ref[...]
    row = cell // (COLS_DEV * col_count) % ROWS_DEV
    place_send[...] = row * COLS_DEV + cell % COLS_DEV

    def encode(tile, dest_ref):
        slot = lax.broadcasted_iota(jnp.int32, (1, cap), 1)
        count = jnp.where(slot < live_ref[tile], count_ref[tile], 0)
        start = pl.multiple_of(tile * cap, cap)
        best = jnp.full((chan, cap), -jnp.inf, jnp.float32)
        for h in range(points // HALF):
            block = x_ref[:, h * HALF : (h + 1) * HALF, pl.ds(start, cap)]
            block = block.reshape(feat * HALF, cap)
            for q in range(HALF // PACK):
                hidden = jnp.dot(w1_ref[q], block, preferred_element_type=jnp.float32)
                hidden = jnp.maximum(hidden + b1_ref[...], 0.0).astype(jnp.bfloat16)
                second = jnp.dot(w2_ref[...], hidden, preferred_element_type=jnp.float32)
                for p in range(PACK):
                    j = h * HALF + q * PACK + p
                    part = second[p * chan : (p + 1) * chan]
                    best = jnp.maximum(best, jnp.where(count > j, part, -jnp.inf))
        vec = jnp.maximum(best + b2_ref[...], 0.0)
        dest_ref[tile] = vec.astype(jnp.bfloat16)

    def place_of(i, slot):
        tile = (me + i) % tiles
        return pltpu.make_async_remote_copy(
            src_ref=place_send.at[tile],
            dst_ref=place_ref.at[slot],
            send_sem=place_ssem.at[i],
            recv_sem=place_rsem.at[i],
            device_id=device_of(tile),
            device_id_type=pl.DeviceIdType.MESH,
        )

    def copy_of(i, slot):
        tile = (me + i) % tiles
        return pltpu.make_async_remote_copy(
            src_ref=send_ref.at[tile],
            dst_ref=out_ref.at[slot],
            send_sem=ssem.at[i],
            recv_sem=rsem.at[i],
            device_id=device_of(tile),
            device_id_type=pl.DeviceIdType.MESH,
        )

    pl.semaphore_wait(barrier, tiles - 1)

    def step(k, carry):
        i = half + (1 - 2 * (k % 2)) * ((k + 1) // 2)
        encode((me + i) % tiles, send_ref)
        copy_of(i, me).start()
        place_of(i, me).start()
        return carry

    lax.fori_loop(0, tiles - 1, step, 0, unroll=3)
    encode(me, out_ref)
    place_ref[me] = place_send[me]

    def finish(i, carry):
        copy_of(i, me).wait_send()
        place_of(i, me).wait_send()
        copy_of(i, (me - i + tiles) % tiles).wait_recv()
        place_of(i, (me - i + tiles) % tiles).wait_recv()
        return carry

    lax.fori_loop(1, tiles, finish, 0)


def encode_all(points, counts, cells, live, embed, mix, bias):
    feat = points.shape[0]
    tiles, _, cap = counts.shape
    chan, mid = mix.shape
    vmem = pl.BlockSpec(memory_space=pltpu.VMEM)
    return pl.pallas_call(
        encode_kernel,
        in_specs=[vmem] * 6 + [pl.BlockSpec(memory_space=pltpu.SMEM)],
        out_specs=[vmem, vmem],
        out_shape=[
            jax.ShapeDtypeStruct((tiles, chan, cap), jnp.bfloat16),
            jax.ShapeDtypeStruct((tiles, 1, cap), jnp.int32),
        ],
        scratch_shapes=[
            pltpu.VMEM((tiles, chan, cap), jnp.bfloat16),
            pltpu.VMEM((tiles, 1, cap), jnp.int32),
            pltpu.VMEM((HALF // PACK, PACK * mid, feat * HALF), jnp.bfloat16),
            pltpu.VMEM((PACK * chan, PACK * mid), jnp.bfloat16),
            pltpu.VMEM((PACK * mid, 1), jnp.float32),
            pltpu.VMEM((chan, 1), jnp.float32),
            pltpu.SemaphoreType.DMA((tiles,)),
            pltpu.SemaphoreType.DMA((tiles,)),
            pltpu.SemaphoreType.DMA((tiles,)),
            pltpu.SemaphoreType.DMA((tiles,)),
        ],
        compiler_params=pltpu.CompilerParams(collective_id=7, has_side_effects=True),
        name="encode_send",
    )(points, counts, cells, embed, mix, bias, live)


def scatter_kernel(cell_ref, vec_ref, out_ref, stage, *grids):
    tiles, chan, cap = vec_ref.shape
    pairs = out_ref.shape[0]
    share = 2 * pairs // tiles

    def prepare(t, carry):
        twice = vec_ref[t].astype(jnp.float32)
        twice = jnp.concatenate([twice, twice], axis=0).T
        stage[pl.ds(pl.multiple_of(t * cap, cap), cap), :] = twice
        for grid in grids:
            grid[pl.ds(pl.multiple_of(t * share, share), share), :] = jnp.zeros(
                (share, 2 * chan), jnp.float32
            )
        return carry

    lax.fori_loop(0, tiles, prepare, 0, unroll=2)
    lanes = len(grids)
    batch = 32

    def scatter(s, carry):
        start = s * batch
        for k in range(0, batch, lanes):
            cells = [cell_ref[start + (k + a)] for a in range(lanes)]
            olds = [grids[a][pl.ds(cells[a], 1), :] for a in range(lanes)]
            news = [stage[pl.ds(start + (k + a), 1), :] for a in range(lanes)]
            for a in range(lanes):
                grids[a][pl.ds(cells[a], 1), :] = jnp.maximum(olds[a], news[a])
        return carry

    lax.fori_loop(0, tiles * cap // batch, scatter, 0)
    part = min(pairs, 256)
    first_half = lax.broadcasted_iota(jnp.int32, (part, 2 * chan), 1) < chan

    def finish(i, carry):
        base = pl.multiple_of(i * 2 * part, 2 * part)
        sides = []
        for side in range(2):
            total = grids[0][pl.ds(base + side, part, stride=2), :]
            for grid in grids[1:]:
                total = jnp.maximum(total, grid[pl.ds(base + side, part, stride=2), :])
            sides.append(total)
        total = jnp.where(first_half, sides[0], sides[1])
        out_ref[pl.ds(pl.multiple_of(i * part, part), part), :] = total.astype(jnp.bfloat16)
        return carry

    lax.fori_loop(0, pairs // part, finish, 0)


def scatter_max(cells, vectors):
    tiles, chan, cap = vectors.shape
    area = ROWS_DEV * COLS_DEV
    return pl.pallas_call(
        scatter_kernel,
        in_specs=[
            pl.BlockSpec(memory_space=pltpu.SMEM),
            pl.BlockSpec(memory_space=pltpu.VMEM),
        ],
        out_specs=pl.BlockSpec(memory_space=pltpu.VMEM),
        out_shape=jax.ShapeDtypeStruct((area // 2, 2 * chan), jnp.bfloat16),
        scratch_shapes=[pltpu.VMEM((tiles * cap, 2 * chan), jnp.float32)]
        + [pltpu.VMEM((area, 2 * chan), jnp.float32)] * LANES,
        name="scatter_max",
    )(cells, vectors)


STEPS = [(dr, dc) for dr in (1, -1) for dc in (0, 1, -1)] + [(0, 1), (0, -1)]


class Halo:
    def __init__(self, stage, own, top, bottom, left, right, send_sem, recv_sem):
        self.stage, self.own = stage, own
        self.top, self.bottom, self.left, self.right = top, bottom, left, right
        self.send_sem, self.recv_sem = send_sem, recv_sem
        self.rows, self.width, _ = own.shape
        self.before, self.after = top.shape[0], bottom.shape[0]
        self.count_rows, self.count_cols = lax.axis_size("row"), lax.axis_size("col")
        self.my_row, self.my_col = lax.axis_index("row"), lax.axis_index("col")
        self.steps = [
            (dr, dc)
            for dr, dc in STEPS
            if (dr == 0 or self.count_rows > 1) and (dc == 0 or self.count_cols > 1)
        ]

    def exists(self, dr, dc):
        row, col = self.my_row + dr, self.my_col + dc
        return (row >= 0) & (row < self.count_rows) & (col >= 0) & (col < self.count_cols)

    def peer(self, dr, dc):
        return {"row": self.my_row + dr, "col": self.my_col + dc}

    def clear(self):
        for ref in (self.top, self.bottom, self.left, self.right):
            ref[...] = jnp.zeros_like(ref)

    def copy_of(self, place):
        dr, dc = self.steps[place]
        before, rows, after = self.before, self.rows, self.after
        row_from = {1: slice(rows - before, rows), 0: slice(0, rows), -1: slice(0, after)}[dr]
        col_from = {1: slice(self.width - SIDE, self.width), 0: slice(0, self.width), -1: slice(0, SIDE)}[dc]
        row_to = {
            1: slice(0, before),
            0: slice(before, before + rows),
            -1: slice(before + rows, before + rows + after),
        }[dr]
        if dc == 0:
            target = self.top if dr == 1 else self.bottom
        else:
            target = (self.left if dc == 1 else self.right).at[row_to]
        return pltpu.make_async_remote_copy(
            src_ref=self.own.at[row_from, col_from, :],
            dst_ref=target,
            send_sem=self.send_sem.at[self.stage, place],
            recv_sem=self.recv_sem.at[self.stage, place],
            device_id=self.peer(dr, dc),
            device_id_type=pl.DeviceIdType.MESH,
        )

    def each(self, keep, sign, action):
        for place, (dr, dc) in enumerate(self.steps):
            if keep(dr, dc):

                @pl.when(self.exists(sign * dr, sign * dc))
                def _():
                    action(self.copy_of(place))

    def start(self, keep):
        self.each(keep, 1, lambda copy: copy.start())

    def wait_send(self):
        self.each(lambda dr, dc: True, 1, lambda copy: copy.wait_send())

    def wait_recv(self, keep):
        self.each(keep, -1, lambda copy: copy.wait_recv())


def across(dr, dc):
    return dr != 0


def beside(dr, dc):
    return dr == 0


def levels_kernel(
    bev_ref, w1a_ref, w1b_ref, w2a_ref, w2b_ref, w3a_ref, w3b_ref, bias_ref,
    one_ref, two_ref, three_ref,
    top0, bottom0, left0, right0, top1, bottom1, left1, right1, top2, bottom2, left2, right2,
    send_sem, recv_sem,
    t1a, t1b, t2a, t2b, t3a, t3b, cat1a, cat1b, cat2e, cat2o, cat2b, cat3e, cat3o, cat3b,
    stage, stage3, stage4,
):
    rows1, pairs, _ = bev_ref.shape
    rows2, cols2, chan2 = two_ref.shape
    rows3, cols3, chan3 = three_ref.shape
    chan1 = w1a_ref.shape[2]
    mid1 = pairs + 16
    mid3 = cols3 + 16
    zero = Halo(0, bev_ref, top0, bottom0, left0, right0, send_sem, recv_sem)
    one = Halo(1, one_ref, top1, bottom1, left1, right1, send_sem, recv_sem)
    two = Halo(2, two_ref, top2, bottom2, left2, right2, send_sem, recv_sem)
    for halo in (zero, one, two):
        halo.clear()
    barrier = pltpu.get_barrier_semaphore()
    for dr, dc in zero.steps:

        @pl.when(zero.exists(dr, dc))
        def _():
            pl.semaphore_signal(
                barrier, inc=1, device_id=zero.peer(dr, dc), device_id_type=pl.DeviceIdType.MESH
            )

    def blocks(w_ref, u):
        wide = [w_ref[u, v].astype(jnp.float32) for v in range(3)]
        nil = jnp.zeros((chan1, chan1), jnp.float32)
        upper = jnp.concatenate([wide[1], wide[0]], axis=0)
        lower = jnp.concatenate([wide[2], wide[1]], axis=0)
        after = jnp.concatenate([nil, wide[2]], axis=0)
        prior = jnp.concatenate([wide[0], nil], axis=0)
        return jnp.concatenate([part.T for part in (upper, lower, after, prior)], axis=0)

    depth = 4 * chan1
    for w_ref, t_ref in ((w1a_ref, t1a), (w1b_ref, t1b)):
        for u in range(3):
            t_ref[u * depth : (u + 1) * depth, :] = blocks(w_ref, u).astype(jnp.bfloat16)

    peers = sum(jnp.where(zero.exists(dr, dc), 1, 0) for dr, dc in zero.steps)
    pl.semaphore_wait(barrier, peers)
    zero.start(lambda dr, dc: True)

    for u in range(3):
        base = u * depth
        t2a[base : base + chan1, :] = w2a_ref[u, 1]
        t2a[base + chan1 : base + 2 * chan1, :] = w2a_ref[u, 2]
        t2a[base + 2 * chan1 : base + 3 * chan1, :] = jnp.zeros((chan1, chan2), jnp.bfloat16)
        t2a[base + 3 * chan1 : base + 4 * chan1, :] = w2a_ref[u, 0]
    for w_ref, t_ref in ((w2b_ref, t2b), (w3a_ref, t3a), (w3b_ref, t3b)):
        deep = w_ref.shape[3]
        for u in range(3):
            for v in range(3):
                flip = w_ref[u, v].astype(jnp.float32).T
                t_ref[(3 * u + v) * deep : (3 * u + v + 1) * deep, :] = flip.astype(jnp.bfloat16)
    stage[...] = jnp.zeros_like(stage)
    stage3[...] = jnp.zeros_like(stage3)
    stage4[...] = jnp.zeros_like(stage4)

    half = lax.broadcasted_iota(jnp.int32, (mid1, TILE), 1) < chan1
    half_own = lax.broadcasted_iota(jnp.int32, (pairs, TILE), 1) < chan1
    has_left, has_right = zero.exists(0, -1), zero.exists(0, 1)
    has_up, has_down = zero.exists(-1, 0), zero.exists(1, 0)
    ways = stage.shape[0]

    def at(i, size):
        return pl.ds(pl.multiple_of(i * size, 16), size)

    def load(halo, r, own_row):
        left = halo.left[r].astype(jnp.float32)
        right = halo.right[r].astype(jnp.float32)
        return left, own_row.astype(jnp.float32), right

    def spread(halo, r, own_row, way):
        left, row, right = load(halo, r, own_row)
        center = jnp.concatenate([left[8:16], row, right[0:8]], axis=0)
        stage[way, 8 : 8 + mid1, :] = center
        return center

    def fill1a(r, own_row, way):
        center = spread(zero, r, own_row, way)
        near = jnp.where(half, stage[way, 9 : 9 + mid1, :], stage[way, 7 : 7 + mid1, :])
        cat1a[at(r, mid1), :] = jnp.concatenate([center, near], axis=1).astype(jnp.bfloat16)

    def fill2a(r, target, own_row, way):
        center = spread(one, r, own_row, way)
        cat_row = jnp.concatenate([center, stage[way, 7 : 7 + mid1, :]], axis=1)
        target[at(r // 2, mid1), :] = cat_row.astype(jnp.bfloat16)

    def fill3a(r, target, own_row, way):
        left, row, right = load(two, r, own_row)
        stage3[way, 8 : 8 + SIDE, :] = left
        stage3[way, 8 + SIDE : 8 + SIDE + cols2, :] = row
        stage3[way, 8 + SIDE + cols2 : 8 + 2 * SIDE + cols2, :] = right
        parts = [stage3[way, pl.ds(7 + v, mid3, stride=2), :] for v in range(3)]
        target[at(r // 2, mid3), :] = jnp.concatenate(parts, axis=1).astype(jnp.bfloat16)

    def bias_of(at_row, times, width):
        return bias_ref[at_row : at_row + 1, 0:width] if times == 1 else None

    bias1a = jnp.concatenate([bias_ref[1:2, 0:chan1]] * 2, axis=1)
    bias1b = jnp.concatenate([bias_ref[1:2, chan1 : 2 * chan1]] * 2, axis=1)
    bias2a, bias2b = bias_ref[2:3, :], bias_ref[3:4, :]
    bias3a = jnp.concatenate([bias_ref[4:5, :], bias_ref[5:6, :]], axis=1)
    bias3b = jnp.concatenate([bias_ref[6:7, :], bias_ref[7:8, :]], axis=1)

    def masked(row, row_good):
        first = jnp.where(has_left & row_good, row[0:8], 0.0)
        last = jnp.where(has_right & row_good, row[row.shape[0] - 8 :], 0.0)
        inner = row[8 : row.shape[0] - 8]
        if row_good is not True:
            inner = jnp.where(row_good, inner, 0.0)
        return jnp.concatenate([first, inner, last], axis=0)

    def conv(lhs, weight, bias):
        total = jnp.dot(jnp.concatenate(lhs, axis=1), weight[...], preferred_element_type=jnp.float32)
        return jnp.maximum(total + bias, 0.0)

    def mid_one(i, count, good):
        lhs = [cat1a[pl.ds(pl.multiple_of((i + u) * mid1, 16), count * mid1), :] for u in range(3)]
        total = conv(lhs, t1a, bias1a)
        for k in range(count):
            row = masked(total[k * mid1 : (k + 1) * mid1], good)
            stage[k, 8 : 8 + mid1, :] = row
            near = jnp.where(half_own, stage[k, 17 : 17 + pairs, :], stage[k, 15 : 15 + pairs, :])
            cat_row = jnp.concatenate([row[8 : 8 + pairs], near], axis=1)
            cat1b[at(i + k, pairs), :] = cat_row.astype(jnp.bfloat16)

    def out_one(i, count):
        lhs = [cat1b[pl.ds(pl.multiple_of((i + u) * pairs, 16), count * pairs), :] for u in range(3)]
        total = conv(lhs, t1b, bias1b).astype(jnp.bfloat16)
        for k in range(count):
            one_ref[i + k] = total[k * pairs : (k + 1) * pairs]

    def mid_two(i, count, good):
        even = [cat2e[pl.ds((i + d) * mid1, count * mid1), :] for d in range(2)]
        odd = cat2o[pl.ds(i * mid1, count * mid1), :]
        total = conv([even[0], odd, even[1]], t2a, bias2a)
        for k in range(count):
            row = masked(total[k * mid1 : (k + 1) * mid1], good)
            stage[k % ways, 8 : 8 + mid1, :] = row
            down = stage[k % ways, 15 : 15 + cols2, :]
            up = stage[k % ways, 17 : 17 + cols2, :]
            cat_row = jnp.concatenate([down, row[8 : 8 + cols2], up], axis=1)
            cat2b[at(i + k, cols2), :] = cat_row.astype(jnp.bfloat16)

    def out_two(i, count):
        lhs = [cat2b[pl.ds((i + u) * cols2, count * cols2), :] for u in range(3)]
        total = conv(lhs, t2b, bias2b).astype(jnp.bfloat16)
        for k in range(count):
            two_ref[i + k] = total[k * cols2 : (k + 1) * cols2]

    def mid_three(i, count, good):
        even = [cat3e[pl.ds((i + d) * mid3, count * mid3), :] for d in range(2)]
        odd = cat3o[pl.ds(i * mid3, count * mid3), :]
        total = conv([even[0], odd, even[1]], t3a, bias3a)
        for k in range(count):
            row = masked(total[k * mid3 : (k + 1) * mid3], good)
            stage4[k % ways, 8 : 8 + mid3, :] = row
            down = stage4[k % ways, 15 : 15 + cols3, :]
            up = stage4[k % ways, 17 : 17 + cols3, :]
            cat_row = jnp.concatenate([down, row[8 : 8 + cols3], up], axis=1)
            cat3b[at(i + k, cols3), :] = cat_row.astype(jnp.bfloat16)

    zero.wait_recv(beside)

    def inner_fill(g, carry):
        for k in range(4):
            r = g * 4 + k
            fill1a(r + 2, bev_ref[r], k)
        return carry

    lax.fori_loop(0, rows1 // 4, inner_fill, 0)

    def inner_mid(g, carry):
        mid_one(2 + g * 2, 2, True)
        return carry

    lax.fori_loop(0, (rows1 - 2) // 2, inner_mid, 0)

    def inner_out(g, carry):
        out_one(2 + g * 2, 2)
        return carry

    lax.fori_loop(0, (rows1 - 4) // 2, inner_out, 0)
    zero.wait_recv(across)
    for k in range(2):
        fill1a(k, top0[k], k)
        fill1a(rows1 + 2 + k, bottom0[k], 2 + k)
    mid_one(0, 1, has_up)
    mid_one(1, 1, True)
    mid_one(rows1, 1, True)
    mid_one(rows1 + 1, 1, has_down)
    out_one(0, 2)
    out_one(rows1 - 2, 2)
    one.start(lambda dr, dc: True)

    one.wait_recv(beside)

    def inner_fill2(g, carry):
        for k in range(2):
            r = g * 4 + 2 * k
            fill2a(r + 3, cat2o, one_ref[r], 2 * k)
            fill2a(r + 4, cat2e, one_ref[r + 1], 2 * k + 1)
        return carry

    lax.fori_loop(0, rows1 // 4, inner_fill2, 0)
    for i in range(2, rows2, 2):
        mid_two(i, 2, True)
    mid_two(rows2, 1, True)
    for i in range(2, rows2 - 2, 2):
        out_two(i, 2)
    out_two(rows2 - 2, 1)
    one.wait_recv(across)
    fill2a(0, cat2e, top1[0], 0)
    fill2a(1, cat2o, top1[1], 1)
    fill2a(2, cat2e, top1[2], 2)
    fill2a(rows1 + 3, cat2o, bottom1[0], 3)
    fill2a(rows1 + 4, cat2e, bottom1[1], 0)
    mid_two(0, 1, has_up)
    mid_two(1, 1, True)
    mid_two(rows2 + 1, 1, has_down)
    out_two(0, 2)
    out_two(rows2 - 1, 1)
    two.start(lambda dr, dc: True)

    two.wait_recv(beside)
    for r in range(rows2):
        fill3a(r + 3, cat3o if r % 2 == 0 else cat3e, two_ref[r], r % ways)
    mid_three(2, rows3 - 1, True)
    two.wait_recv(across)
    fill3a(0, cat3e, top2[0], 0)
    fill3a(1, cat3o, top2[1], 1)
    fill3a(2, cat3e, top2[2], 2)
    fill3a(rows2 + 3, cat3o, bottom2[0], 3)
    fill3a(rows2 + 4, cat3e, bottom2[1], 0)
    mid_three(0, 1, has_up)
    mid_three(1, 1, True)
    mid_three(rows3 + 1, 1, has_down)
    lhs = [cat3b[u * cols3 : (u + rows3) * cols3, :] for u in range(3)]
    total = conv(lhs, t3b, bias3b).astype(jnp.bfloat16)
    three_ref[...] = total.reshape(rows3, cols3, chan3)
    for halo in (zero, one, two):
        halo.wait_send()


def levels(bev, convs, bias):
    rows1, pairs, _ = bev.shape
    w1a, w1b, w2a, w2b, w3a, w3b = convs
    chan1, chan2, chan3 = w1a.shape[2], w2b.shape[2], w3b.shape[2]
    rows2, rows3, cols2, cols3 = rows1 // 2, rows1 // 4, pairs, pairs // 2
    vmem = pl.BlockSpec(memory_space=pltpu.VMEM)
    mid1, mid3 = pairs + 16, cols3 + 16

    def buffers(rows, before, after):
        return [
            pltpu.VMEM((before, pairs, TILE), jnp.bfloat16),
            pltpu.VMEM((after, pairs, TILE), jnp.bfloat16),
            pltpu.VMEM((before + rows + after, SIDE, TILE), jnp.bfloat16),
            pltpu.VMEM((before + rows + after, SIDE, TILE), jnp.bfloat16),
        ]

    def half(*shape):
        return pltpu.VMEM(shape, jnp.bfloat16)

    return pl.pallas_call(
        levels_kernel,
        in_specs=[vmem] * 8,
        out_specs=[vmem] * 3,
        out_shape=[
            jax.ShapeDtypeStruct((rows1, pairs, TILE), jnp.bfloat16),
            jax.ShapeDtypeStruct((rows2, cols2, chan2), jnp.bfloat16),
            jax.ShapeDtypeStruct((rows3, cols3, chan3), jnp.bfloat16),
        ],
        scratch_shapes=buffers(rows1, 2, 2)
        + buffers(rows1, 3, 2)
        + buffers(rows2, 3, 2)
        + [pltpu.SemaphoreType.DMA((3, len(STEPS)))] * 2
        + [
            half(12 * chan1, 2 * chan1),
            half(12 * chan1, 2 * chan1),
            half(12 * chan1, chan2),
            half(9 * chan2, chan2),
            half(9 * chan2, chan3),
            half(9 * chan3, chan3),
            half((rows1 + 4) * mid1, 4 * chan1),
            half((rows1 + 2) * pairs, 4 * chan1),
            half((rows2 + 3) * mid1, 4 * chan1),
            half((rows2 + 2) * mid1, 4 * chan1),
            half((rows2 + 2) * cols2, 3 * chan2),
            half((rows3 + 3) * mid3, 3 * chan2),
            half((rows3 + 2) * mid3, 3 * chan2),
            half((rows3 + 2) * cols3, 3 * chan3),
            pltpu.VMEM((4, mid1 + 16, TILE), jnp.float32),
            pltpu.VMEM((4, cols2 + 2 * SIDE + 16, TILE), jnp.float32),
            pltpu.VMEM((4, mid3 + 16, chan3), jnp.float32),
        ],
        compiler_params=pltpu.CompilerParams(collective_id=8, has_side_effects=True),
        name="levels",
    )(bev, *convs, bias)


def lift_kernel(
    one_ref, two_ref, three_ref, near_ref, mid_ref, far_ref, bias_ref, out_ref,
    result, expand1, expand2, expand3, gather, sem,
):
    rows, pairs, _ = one_ref.shape
    up = near_ref.shape[1]
    cols = 2 * pairs
    near = near_ref[...].astype(jnp.float32)
    near = jnp.concatenate([near, near], axis=0).T.astype(jnp.bfloat16)
    expand2[...] = jnp.zeros_like(expand2)
    expand3[...] = jnp.zeros_like(expand3)
    first_half = lax.broadcasted_iota(jnp.int32, (pairs, TILE), 1) < TILE // 2

    def product(weight, wide):
        return lax.dot_general(
            weight, wide, (((1,), (1,)), ((), ())), preferred_element_type=jnp.float32
        )

    def put(row, value, bias):
        for h in range(cols // TILE):
            piece = jnp.maximum(value[:, h * TILE : (h + 1) * TILE] + bias, 0.0)
            gather[h, pl.ds(row, up, stride=rows), :] = piece

    def finish(which):
        for h in range(cols // TILE):
            done = gather[h].astype(jnp.bfloat16).reshape(up, rows, TILE)
            result[which, :, :, h * TILE : (h + 1) * TILE] = done
        pltpu.make_async_copy(
            result.at[which], out_ref.at[pl.ds(which * up, up)], sem.at[which]
        ).start()

    def bias_tile(at_row):
        return jnp.broadcast_to(bias_ref[at_row : at_row + 1, :], (TILE, up)).T

    bias = bias_tile(8)
    for r in range(rows):
        row = one_ref[r].astype(jnp.float32)
        way = r % 2
        expand1[way, pl.ds(0, pairs, stride=2), :] = jnp.where(first_half, row, 0.0)
        expand1[way, pl.ds(1, pairs, stride=2), :] = jnp.where(first_half, 0.0, row)
        put(r, product(near, expand1[way].astype(jnp.bfloat16)), bias)
    finish(0)

    bias = bias_tile(9)
    factor = mid_ref.shape[0]
    weight = [
        jnp.concatenate([mid_ref[a, e] for e in range(factor)], axis=1) for a in range(factor)
    ]
    weight = jnp.concatenate(weight, axis=0)
    for i in range(two_ref.shape[0]):
        row = two_ref[i].astype(jnp.float32)
        way = i % 2
        for e in range(factor):
            expand2[way, e, pl.ds(e, row.shape[0], stride=factor), :] = row
        wide = jnp.concatenate([expand2[way, e] for e in range(factor)], axis=1)
        total = product(weight, wide.astype(jnp.bfloat16))
        for a in range(factor):
            put(i * factor + a, total[a * up : (a + 1) * up], bias)
    finish(1)

    bias = bias_tile(10)
    factor = far_ref.shape[0]
    weight = [
        jnp.concatenate([far_ref[a, e] for e in range(factor)], axis=1) for a in range(factor)
    ]
    weight = jnp.concatenate(weight, axis=0)
    halves = three_ref.shape[2] // TILE
    for i in range(three_ref.shape[0]):
        row = three_ref[i].astype(jnp.float32)
        for e in range(factor):
            for h in range(halves):
                expand3[e * halves + h, pl.ds(e, row.shape[0], stride=factor), :] = row[
                    :, h * TILE : (h + 1) * TILE
                ]
        wide = jnp.concatenate([expand3[k] for k in range(factor * halves)], axis=1)
        total = product(weight, wide.astype(jnp.bfloat16))
        for a in range(factor):
            put(i * factor + a, total[a * up : (a + 1) * up], bias)
    finish(2)
    for which in range(3):
        pltpu.make_async_copy(
            result.at[which], out_ref.at[pl.ds(which * up, up)], sem.at[which]
        ).wait()


def lifts(maps, weights, bias):
    rows, pairs, _ = maps[0].shape
    near, mid, far = weights
    up = near.shape[1]
    cols = 2 * pairs
    vmem = pl.BlockSpec(memory_space=pltpu.VMEM)
    factor, halves = far.shape[0], far.shape[3] // TILE
    return pl.pallas_call(
        lift_kernel,
        in_specs=[vmem] * 7,
        out_specs=pl.BlockSpec(memory_space=pl.ANY),
        out_shape=jax.ShapeDtypeStruct((3 * up, rows, cols), jnp.bfloat16),
        scratch_shapes=[
            pltpu.VMEM((3, up, rows, cols), jnp.bfloat16),
            pltpu.VMEM((2, cols, TILE), jnp.float32),
            pltpu.VMEM((2, mid.shape[0], cols, TILE), jnp.float32),
            pltpu.VMEM((factor * halves, cols, TILE), jnp.float32),
            pltpu.VMEM((cols // TILE, up * rows, TILE), jnp.float32),
            pltpu.SemaphoreType.DMA((3,)),
        ],
        name="lifts",
    )(*maps, near, mid, far, bias)


def on_device(
    points,
    pillar_cell,
    point_count,
    tile_count,
    point_embed,
    point_mix,
    first_conv,
    second_conv,
    third_conv,
    fourth_conv,
    fifth_conv,
    sixth_conv,
    near_lift,
    mid_lift,
    far_lift,
    biases,
):
    tile_num = tile_count.shape[0]
    capacity = points.shape[2] // tile_num
    bias = biases.reshape(-1, TILE)
    vectors, places = encode_all(
        points,
        point_count.reshape(tile_num, 1, capacity),
        pillar_cell.reshape(tile_num, 1, capacity),
        tile_count,
        jnp.transpose(point_embed),
        point_mix,
        bias,
    )
    chan = point_mix.shape[0]
    bev = scatter_max(places.reshape(-1), vectors)
    bev = bev.reshape(ROWS_DEV, COLS_DEV // 2, 2 * chan)
    convs = (
        first_conv,
        second_conv,
        jnp.transpose(third_conv, (0, 1, 3, 2)),
        fourth_conv,
        fifth_conv,
        sixth_conv,
    )
    maps = levels(bev, convs, bias)
    near = jnp.transpose(near_lift, (0, 1, 3, 2)).reshape(near_lift.shape[3], near_lift.shape[2])
    return lifts(maps, (near, mid_lift, far_lift), bias)


def solution(mesh):
    return jax.shard_map(
        on_device,
        mesh=mesh,
        in_specs=(
            P(None, None, ("slab", "row", "col")),
            P(("slab", "row", "col")),
            P(("slab", "row", "col")),
            P(("slab", "row", "col")),
            P(),
            P(),
            P(),
            P(),
            P(),
            P(),
            P(),
            P(),
            P(),
            P(),
            P(),
            P(),
        ),
        out_specs=P(None, ("slab", "row"), "col"),
        check_vma=False,
    )
```

```python
import jax
import jax.numpy as jnp
from jax import lax
from jax.experimental import pallas as pl
from jax.experimental.pallas import tpu as pltpu
from jax.sharding import PartitionSpec as P

ROWS_DEV = 16
COLS_DEV = 256
PACK = 4
HALF = 16
LANES = 4
SIDE = 16
TILE = 128


def encode_kernel(
    x_ref, count_ref, cell_ref, embed_ref, mix_ref, bias_ref, live_ref, out_ref, place_ref,
    x_tiles, send_ref, place_send, w1_ref, w2_ref, b1_ref, b2_ref, x_sem, ssem, rsem,
    place_ssem, place_rsem
):
    feat, points, _ = x_ref.shape
    tiles, _, cap = count_ref.shape
    chan, mid = mix_ref.shape
    half = tiles // 2
    col_count = lax.axis_size("col")
    me = lax.axis_index("row") * col_count + lax.axis_index("col")

    side, rank = me // half, me % half

    def device_of(tile):
        return {"row": tile // col_count, "col": tile % col_count}

    def tile_of(k):
        own = k // half
        return (side + 1 + own) % 2 * half + (rank + k + own) % half

    def source_of(k):
        own = k // half
        return (side + 1 + own) % 2 * half + (rank - k - own + 2 * half) % half

    def fetch(tile):
        start = pl.multiple_of(tile * cap, cap)
        return pltpu.make_async_copy(
            x_ref.at[:, :, pl.ds(start, cap)], x_tiles.at[tile], x_sem.at[tile]
        )

    def fetch_start(k, carry):
        fetch(tile_of(k)).start()
        return carry

    lax.fori_loop(0, tiles - 1, fetch_start, 0)
    fetch(me).start()
    barrier = pltpu.get_barrier_semaphore()

    def greet(i, carry):
        pl.semaphore_signal(
            barrier,
            inc=1,
            device_id=device_of((me + i) % tiles),
            device_id_type=pl.DeviceIdType.MESH,
        )
        return carry

    lax.fori_loop(1, tiles, greet, 0)

    wide = feat * HALF
    lane = lax.broadcasted_iota(jnp.int32, (feat, wide), 1)
    spread = lane // HALF == lax.broadcasted_iota(jnp.int32, (feat, wide), 0)
    spread = jnp.where(spread, 1.0, 0.0).astype(jnp.bfloat16)
    full = lax.dot_general(
        embed_ref[...], spread, (((0,), (0,)), ((), ())), preferred_element_type=jnp.float32
    )
    point = lax.broadcasted_iota(jnp.int32, (mid, wide), 1) % HALF
    for q in range(HALF // PACK):
        for p in range(PACK):
            part = jnp.where(point == q * PACK + p, full, 0.0)
            w1_ref[q, p * mid : (p + 1) * mid, :] = part.astype(jnp.bfloat16)
    w2_ref[...] = jnp.zeros_like(w2_ref)
    for p in range(PACK):
        w2_ref[p * chan : (p + 1) * chan, p * mid : (p + 1) * mid] = mix_ref[...]
    both = mid + chan
    column = jnp.broadcast_to(bias_ref[0:1, :], (both, both)).T[:, 0:1]
    for p in range(PACK):
        b1_ref[p * mid : (p + 1) * mid, :] = column[0:mid]
    b2_ref[...] = column[mid:both]
    cell = cell_ref[...]
    row = cell // (COLS_DEV * col_count) % ROWS_DEV
    place_send[...] = row * COLS_DEV + cell % COLS_DEV

    def encode(tile, dest_ref):
        slot = lax.broadcasted_iota(jnp.int32, (1, cap), 1)
        count = jnp.where(slot < live_ref[tile], count_ref[tile], 0)
        fetch(tile).wait()
        best = jnp.full((chan, cap), -jnp.inf, jnp.float32)
        for h in range(points // HALF):
            block = x_tiles[tile, :, h * HALF : (h + 1) * HALF, :]
            block = block.reshape(feat * HALF, cap)
            for q in range(HALF // PACK):
                hidden = jnp.dot(w1_ref[q], block, preferred_element_type=jnp.float32)
                hidden = jnp.maximum(hidden + b1_ref[...], 0.0).astype(jnp.bfloat16)
                second = jnp.dot(w2_ref[...], hidden, preferred_element_type=jnp.float32)
                for p in range(PACK):
                    j = h * HALF + q * PACK + p
                    part = second[p * chan : (p + 1) * chan]
                    best = jnp.maximum(best, jnp.where(count > j, part, -jnp.inf))
        vec = jnp.maximum(best + b2_ref[...], 0.0)
        dest_ref[tile] = vec.astype(jnp.bfloat16)

    def copy_of(k, source, target, send_sem, recv_sem):
        return pltpu.make_async_remote_copy(
            src_ref=source.at[tile_of(k)],
            dst_ref=target,
            send_sem=send_sem.at[k],
            recv_sem=recv_sem.at[k],
            device_id=device_of(tile_of(k)),
            device_id_type=pl.DeviceIdType.MESH,
        )

    def copies(k, slot):
        return [
            copy_of(k, send_ref, out_ref.at[slot], ssem, rsem),
            copy_of(k, place_send, place_ref.at[slot], place_ssem, place_rsem),
        ]

    pl.semaphore_wait(barrier, tiles - 1)

    def step(k, carry):
        encode(tile_of(k), send_ref)
        for copy in copies(k, me):
            copy.start()
        return carry

    lax.fori_loop(0, tiles - 1, step, 0, unroll=3)
    encode(me, out_ref)
    place_ref[me] = place_send[me]

    def finish(k, carry):
        for copy in copies(k, me):
            copy.wait_send()
        for copy in copies(k, source_of(k)):
            copy.wait_recv()
        return carry

    lax.fori_loop(0, tiles - 1, finish, 0)


def encode_all(points, counts, cells, live, embed, mix, bias):
    feat, depth, _ = points.shape
    tiles, _, cap = counts.shape
    chan, mid = mix.shape
    vmem = pl.BlockSpec(memory_space=pltpu.VMEM)
    return pl.pallas_call(
        encode_kernel,
        in_specs=[pl.BlockSpec(memory_space=pl.ANY)]
        + [vmem] * 5
        + [pl.BlockSpec(memory_space=pltpu.SMEM)],
        out_specs=[vmem, vmem],
        out_shape=[
            jax.ShapeDtypeStruct((tiles, chan, cap), jnp.bfloat16),
            jax.ShapeDtypeStruct((tiles, 1, cap), jnp.int32),
        ],
        scratch_shapes=[
            pltpu.VMEM((tiles, feat, depth, cap), jnp.bfloat16),
            pltpu.VMEM((tiles, chan, cap), jnp.bfloat16),
            pltpu.VMEM((tiles, 1, cap), jnp.int32),
            pltpu.VMEM((HALF // PACK, PACK * mid, feat * HALF), jnp.bfloat16),
            pltpu.VMEM((PACK * chan, PACK * mid), jnp.bfloat16),
            pltpu.VMEM((PACK * mid, 1), jnp.float32),
            pltpu.VMEM((chan, 1), jnp.float32),
            pltpu.SemaphoreType.DMA((tiles,)),
            pltpu.SemaphoreType.DMA((tiles,)),
            pltpu.SemaphoreType.DMA((tiles,)),
            pltpu.SemaphoreType.DMA((tiles,)),
            pltpu.SemaphoreType.DMA((tiles,)),
        ],
        compiler_params=pltpu.CompilerParams(collective_id=7, has_side_effects=True),
        name="encode_send",
    )(points, counts, cells, embed, mix, bias, live)


def scatter_kernel(cell_ref, vec_ref, out_ref, stage, *grids):
    tiles, chan, cap = vec_ref.shape
    pairs = out_ref.shape[0]
    share = 2 * pairs // tiles

    def prepare(t, carry):
        twice = vec_ref[t].astype(jnp.float32)
        twice = jnp.concatenate([twice, twice], axis=0).T
        stage[pl.ds(pl.multiple_of(t * cap, cap), cap), :] = twice
        for grid in grids:
            grid[pl.ds(pl.multiple_of(t * share, share), share), :] = jnp.zeros(
                (share, 2 * chan), jnp.float32
            )
        return carry

    lax.fori_loop(0, tiles, prepare, 0, unroll=2)
    lanes = len(grids)
    batch = 64

    def scatter(s, carry):
        start = s * batch
        for k in range(0, batch, lanes):
            cells = [cell_ref[start + (k + a)] for a in range(lanes)]
            olds = [grids[a][pl.ds(cells[a], 1), :] for a in range(lanes)]
            news = [stage[pl.ds(start + (k + a), 1), :] for a in range(lanes)]
            for a in range(lanes):
                grids[a][pl.ds(cells[a], 1), :] = jnp.maximum(olds[a], news[a])
        return carry

    lax.fori_loop(0, tiles * cap // batch, scatter, 0)
    part = min(pairs, 256)
    first_half = lax.broadcasted_iota(jnp.int32, (part, 2 * chan), 1) < chan

    def finish(i, carry):
        base = pl.multiple_of(i * 2 * part, 2 * part)
        sides = []
        for side in range(2):
            total = grids[0][pl.ds(base + side, part, stride=2), :]
            for grid in grids[1:]:
                total = jnp.maximum(total, grid[pl.ds(base + side, part, stride=2), :])
            sides.append(total)
        total = jnp.where(first_half, sides[0], sides[1])
        out_ref[pl.ds(pl.multiple_of(i * part, part), part), :] = total.astype(jnp.bfloat16)
        return carry

    lax.fori_loop(0, pairs // part, finish, 0)


def scatter_max(cells, vectors):
    tiles, chan, cap = vectors.shape
    area = ROWS_DEV * COLS_DEV
    return pl.pallas_call(
        scatter_kernel,
        in_specs=[
            pl.BlockSpec(memory_space=pltpu.SMEM),
            pl.BlockSpec(memory_space=pltpu.VMEM),
        ],
        out_specs=pl.BlockSpec(memory_space=pltpu.VMEM),
        out_shape=jax.ShapeDtypeStruct((area // 2, 2 * chan), jnp.bfloat16),
        scratch_shapes=[pltpu.VMEM((tiles * cap, 2 * chan), jnp.float32)]
        + [pltpu.VMEM((area, 2 * chan), jnp.float32)] * LANES,
        name="scatter_max",
    )(cells, vectors)


STEPS = [(dr, dc) for dr in (1, -1) for dc in (0, 1, -1)] + [(0, 1), (0, -1)]


class Halo:
    def __init__(self, stage, own, top, bottom, left, right, send_sem, recv_sem):
        self.stage, self.own = stage, own
        self.top, self.bottom, self.left, self.right = top, bottom, left, right
        self.send_sem, self.recv_sem = send_sem, recv_sem
        self.rows, self.width, _ = own.shape
        self.before, self.after = top.shape[0], bottom.shape[0]
        self.count_rows, self.count_cols = lax.axis_size("row"), lax.axis_size("col")
        self.my_row, self.my_col = lax.axis_index("row"), lax.axis_index("col")
        self.steps = [
            (dr, dc)
            for dr, dc in STEPS
            if (dr == 0 or self.count_rows > 1) and (dc == 0 or self.count_cols > 1)
        ]

    def exists(self, dr, dc):
        row, col = self.my_row + dr, self.my_col + dc
        return (row >= 0) & (row < self.count_rows) & (col >= 0) & (col < self.count_cols)

    def peer(self, dr, dc):
        return {"row": self.my_row + dr, "col": self.my_col + dc}

    def clear(self):
        for ref in (self.top, self.bottom, self.left, self.right):
            ref[...] = jnp.zeros_like(ref)

    def copy_of(self, place):
        dr, dc = self.steps[place]
        before, rows, after = self.before, self.rows, self.after
        row_from = {1: slice(rows - before, rows), 0: slice(0, rows), -1: slice(0, after)}[dr]
        col_from = {1: slice(self.width - SIDE, self.width), 0: slice(0, self.width), -1: slice(0, SIDE)}[dc]
        row_to = {
            1: slice(0, before),
            0: slice(before, before + rows),
            -1: slice(before + rows, before + rows + after),
        }[dr]
        if dc == 0:
            target = self.top if dr == 1 else self.bottom
        else:
            target = (self.left if dc == 1 else self.right).at[row_to]
        return pltpu.make_async_remote_copy(
            src_ref=self.own.at[row_from, col_from, :],
            dst_ref=target,
            send_sem=self.send_sem.at[self.stage, place],
            recv_sem=self.recv_sem.at[self.stage, place],
            device_id=self.peer(dr, dc),
            device_id_type=pl.DeviceIdType.MESH,
        )

    def each(self, keep, sign, action):
        for place, (dr, dc) in enumerate(self.steps):
            if keep(dr, dc):

                @pl.when(self.exists(sign * dr, sign * dc))
                def _():
                    action(self.copy_of(place))

    def start(self, keep):
        self.each(keep, 1, lambda copy: copy.start())

    def wait_send(self):
        self.each(lambda dr, dc: True, 1, lambda copy: copy.wait_send())

    def wait_recv(self, keep):
        self.each(keep, -1, lambda copy: copy.wait_recv())


def across(dr, dc):
    return dr != 0


def beside(dr, dc):
    return dr == 0


def product(weight, wide_row):
    return lax.dot_general(
        weight, wide_row, (((1,), (1,)), ((), ())), preferred_element_type=jnp.float32
    )


def put_row(gather, rows, row, value, bias):
    for h in range(gather.shape[0]):
        piece = jnp.maximum(value[:, h * TILE : (h + 1) * TILE] + bias, 0.0)
        gather[h, pl.ds(row, value.shape[0], stride=rows), :] = piece


def take_rows(gather, rows, target):
    for h in range(gather.shape[0]):
        done = gather[h].astype(jnp.bfloat16).reshape(-1, rows, TILE)
        target[:, :, h * TILE : (h + 1) * TILE] = done


def stacked(w_ref):
    factor = w_ref.shape[0]
    weight = [jnp.concatenate([w_ref[a, e] for e in range(factor)], axis=1) for a in range(factor)]
    return jnp.concatenate(weight, axis=0)


def far_kernel(
    upper_hbm, three_hbm, far_hbm, bias_hbm, out_ref,
    upper, three_ref, far_ref, bias_ref, result, expand, gather, load_sem, out_sem,
):
    up, rows, _ = result.shape
    pieces = upper.shape[0] // up
    loads = [
        pltpu.make_async_copy(source, target, load_sem.at[place])
        for place, (source, target) in enumerate(
            [(three_hbm, three_ref), (bias_hbm, bias_ref), (far_hbm, far_ref)]
        )
    ]
    passing = [
        (
            pltpu.make_async_copy(
                upper_hbm.at[pl.ds(k * up, up)], upper.at[pl.ds(k * up, up)], load_sem.at[3 + k]
            ),
            pltpu.make_async_copy(
                upper.at[pl.ds(k * up, up)], out_ref.at[pl.ds(k * up, up)], out_sem.at[k]
            ),
        )
        for k in range(pieces)
    ]
    for copy in loads:
        copy.start()
    for copy_in, _ in passing:
        copy_in.start()
    expand[...] = jnp.zeros_like(expand)
    for copy in loads:
        copy.wait()
    last = bias_ref.shape[0] - 1
    bias = jnp.broadcast_to(bias_ref[last : last + 1, :], (TILE, up)).T
    factor = far_ref.shape[0]
    rows3, cols3, chan3 = three_ref.shape
    weight = stacked(far_ref)
    halves = chan3 // TILE
    for i in range(rows3):
        row = three_ref[i].astype(jnp.float32)
        for e in range(factor):
            for h in range(halves):
                piece = row[:, h * TILE : (h + 1) * TILE]
                expand[e * halves + h, pl.ds(e, cols3, stride=factor), :] = piece
        wide_row = jnp.concatenate([expand[k] for k in range(factor * halves)], axis=1)
        total = product(weight, wide_row.astype(jnp.bfloat16))
        for a in range(factor):
            put_row(gather, rows, i * factor + a, total[a * up : (a + 1) * up], bias)
        if i < pieces:
            passing[i][0].wait()
            passing[i][1].start()
    take_rows(gather, rows, result)
    final = pltpu.make_async_copy(result, out_ref.at[pl.ds(pieces * up, up)], out_sem.at[pieces])
    final.start()
    for _, copy_out in passing:
        copy_out.wait()
    final.wait()


def far_lift_all(upper, three, far, bias):
    up = far.shape[2]
    two_up, rows, cols = upper.shape
    operands = (upper, three, far, bias)
    return pl.pallas_call(
        far_kernel,
        in_specs=[pl.BlockSpec(memory_space=pl.ANY)] * len(operands),
        out_specs=pl.BlockSpec(memory_space=pl.ANY),
        out_shape=jax.ShapeDtypeStruct((two_up + up, rows, cols), jnp.bfloat16),
        scratch_shapes=[pltpu.VMEM(operand.shape, operand.dtype) for operand in operands]
        + [
            pltpu.VMEM((up, rows, cols), jnp.bfloat16),
            pltpu.VMEM((far.shape[0] * far.shape[3] // TILE, cols, TILE), jnp.float32),
            pltpu.VMEM((cols // TILE, up * rows, TILE), jnp.float32),
            pltpu.SemaphoreType.DMA((3 + two_up // up,)),
            pltpu.SemaphoreType.DMA((1 + two_up // up,)),
        ],
        name="far_lift",
    )(*operands)


def levels_kernel(
    bev_hbm, w1a_hbm, w1b_hbm, w2a_hbm, w2b_hbm, w3a_hbm, w3b_hbm, near_hbm, mid_hbm, bias_hbm,
    out_ref, three_hbm,
    bev_ref, w1a_ref, w1b_ref, w2a_ref, w2b_ref, w3a_ref, w3b_ref, near_ref, mid_ref, bias_ref,
    load_sem, one_ref, two_ref, three_ref,
    top0, bottom0, left0, right0, top1, bottom1, left1, right1, top2, bottom2, left2, right2,
    send_sem, recv_sem,
    t1a, t1b, t2a, t2b, t3a, t3b, cat1a, cat1b, cat2e, cat2o, cat2b, cat3e, cat3o, cat3b,
    stage, stage3, stage4, result, expand1, expand2, gather, out_sem,
):
    loads = [
        pltpu.make_async_copy(source, target, load_sem.at[place])
        for place, (source, target) in enumerate(
            [
                (bev_hbm, bev_ref),
                (bias_hbm, bias_ref),
                (w1a_hbm, w1a_ref),
                (w1b_hbm, w1b_ref),
                (w2a_hbm, w2a_ref),
                (w2b_hbm, w2b_ref),
                (w3a_hbm, w3a_ref),
                (w3b_hbm, w3b_ref),
                (near_hbm, near_ref),
                (mid_hbm, mid_ref),
            ]
        )
    ]
    for copy in loads:
        copy.start()
    rows1, pairs, _ = bev_ref.shape
    rows2, cols2, chan2 = two_ref.shape
    rows3, cols3, chan3 = three_ref.shape
    chan1 = w1a_ref.shape[2]
    mid1 = pairs + 16
    mid3 = cols3 + 16
    zero = Halo(0, bev_hbm, top0, bottom0, left0, right0, send_sem, recv_sem)
    one = Halo(1, one_ref, top1, bottom1, left1, right1, send_sem, recv_sem)
    two = Halo(2, two_ref, top2, bottom2, left2, right2, send_sem, recv_sem)
    for halo in (zero, one, two):
        halo.clear()
    barrier = pltpu.get_barrier_semaphore()
    for dr, dc in zero.steps:

        @pl.when(zero.exists(dr, dc))
        def _():
            pl.semaphore_signal(
                barrier, inc=1, device_id=zero.peer(dr, dc), device_id_type=pl.DeviceIdType.MESH
            )

    def blocks(w_ref, u):
        wide = [w_ref[u, v].astype(jnp.float32) for v in range(3)]
        nil = jnp.zeros((chan1, chan1), jnp.float32)
        upper = jnp.concatenate([wide[1], wide[0]], axis=0)
        lower = jnp.concatenate([wide[2], wide[1]], axis=0)
        after = jnp.concatenate([nil, wide[2]], axis=0)
        prior = jnp.concatenate([wide[0], nil], axis=0)
        return jnp.concatenate([part.T for part in (upper, lower, after, prior)], axis=0)

    peers = sum(jnp.where(zero.exists(dr, dc), 1, 0) for dr, dc in zero.steps)
    pl.semaphore_wait(barrier, peers)
    zero.start(lambda dr, dc: True)

    for copy in loads[0:4]:
        copy.wait()
    depth = 4 * chan1
    for w_ref, t_ref in ((w1a_ref, t1a), (w1b_ref, t1b)):
        for u in range(3):
            t_ref[u * depth : (u + 1) * depth, :] = blocks(w_ref, u).astype(jnp.bfloat16)

    for copy in loads[4:8]:
        copy.wait()
    for u in range(3):
        base = u * depth
        t2a[base : base + chan1, :] = w2a_ref[u, 1]
        t2a[base + chan1 : base + 2 * chan1, :] = w2a_ref[u, 2]
        t2a[base + 2 * chan1 : base + 3 * chan1, :] = jnp.zeros((chan1, chan2), jnp.bfloat16)
        t2a[base + 3 * chan1 : base + 4 * chan1, :] = w2a_ref[u, 0]
    for w_ref, t_ref in ((w2b_ref, t2b), (w3a_ref, t3a), (w3b_ref, t3b)):
        deep = w_ref.shape[3]
        for u in range(3):
            for v in range(3):
                flip = w_ref[u, v].astype(jnp.float32).T
                t_ref[(3 * u + v) * deep : (3 * u + v + 1) * deep, :] = flip.astype(jnp.bfloat16)
    stage[...] = jnp.zeros_like(stage)
    stage3[...] = jnp.zeros_like(stage3)
    stage4[...] = jnp.zeros_like(stage4)

    half = lax.broadcasted_iota(jnp.int32, (mid1, TILE), 1) < chan1
    half_own = lax.broadcasted_iota(jnp.int32, (pairs, TILE), 1) < chan1
    has_left, has_right = zero.exists(0, -1), zero.exists(0, 1)
    has_up, has_down = zero.exists(-1, 0), zero.exists(1, 0)
    ways = stage.shape[0]

    def at(i, size):
        return pl.ds(pl.multiple_of(i * size, 16), size)

    def load(halo, r, own_row):
        left = halo.left[r].astype(jnp.float32)
        right = halo.right[r].astype(jnp.float32)
        return left, own_row.astype(jnp.float32), right

    def spread(halo, r, own_row, way):
        left, row, right = load(halo, r, own_row)
        center = jnp.concatenate([left[8:16], row, right[0:8]], axis=0)
        stage[way, 8 : 8 + mid1, :] = center
        return center

    def fill1a(r, own_row, way):
        center = spread(zero, r, own_row, way)
        near = jnp.where(half, stage[way, 9 : 9 + mid1, :], stage[way, 7 : 7 + mid1, :])
        cat1a[at(r, mid1), :] = jnp.concatenate([center, near], axis=1).astype(jnp.bfloat16)

    def fill2a(r, target, own_row, way):
        center = spread(one, r, own_row, way)
        cat_row = jnp.concatenate([center, stage[way, 7 : 7 + mid1, :]], axis=1)
        target[at(r // 2, mid1), :] = cat_row.astype(jnp.bfloat16)

    def fill3a(r, target, own_row, way):
        left, row, right = load(two, r, own_row)
        stage3[way, 8 : 8 + SIDE, :] = left
        stage3[way, 8 + SIDE : 8 + SIDE + cols2, :] = row
        stage3[way, 8 + SIDE + cols2 : 8 + 2 * SIDE + cols2, :] = right
        parts = [stage3[way, pl.ds(7 + v, mid3, stride=2), :] for v in range(3)]
        target[at(r // 2, mid3), :] = jnp.concatenate(parts, axis=1).astype(jnp.bfloat16)

    def bias_of(at_row, times, width):
        return bias_ref[at_row : at_row + 1, 0:width] if times == 1 else None

    bias1a = jnp.concatenate([bias_ref[1:2, 0:chan1]] * 2, axis=1)
    bias1b = jnp.concatenate([bias_ref[1:2, chan1 : 2 * chan1]] * 2, axis=1)
    bias2a, bias2b = bias_ref[2:3, :], bias_ref[3:4, :]
    bias3a = jnp.concatenate([bias_ref[4:5, :], bias_ref[5:6, :]], axis=1)
    bias3b = jnp.concatenate([bias_ref[6:7, :], bias_ref[7:8, :]], axis=1)

    def masked(row, row_good):
        first = jnp.where(has_left & row_good, row[0:8], 0.0)
        last = jnp.where(has_right & row_good, row[row.shape[0] - 8 :], 0.0)
        inner = row[8 : row.shape[0] - 8]
        if row_good is not True:
            inner = jnp.where(row_good, inner, 0.0)
        return jnp.concatenate([first, inner, last], axis=0)

    def conv(lhs, weight, bias):
        total = jnp.dot(jnp.concatenate(lhs, axis=1), weight[...], preferred_element_type=jnp.float32)
        return jnp.maximum(total + bias, 0.0)

    def mid_one(i, count, good):
        lhs = [cat1a[pl.ds(pl.multiple_of((i + u) * mid1, 16), count * mid1), :] for u in range(3)]
        total = conv(lhs, t1a, bias1a)
        for k in range(count):
            row = masked(total[k * mid1 : (k + 1) * mid1], good)
            stage[k, 8 : 8 + mid1, :] = row
            near = jnp.where(half_own, stage[k, 17 : 17 + pairs, :], stage[k, 15 : 15 + pairs, :])
            cat_row = jnp.concatenate([row[8 : 8 + pairs], near], axis=1)
            cat1b[at(i + k, pairs), :] = cat_row.astype(jnp.bfloat16)

    def out_one(i, count):
        lhs = [cat1b[pl.ds(pl.multiple_of((i + u) * pairs, 16), count * pairs), :] for u in range(3)]
        total = conv(lhs, t1b, bias1b).astype(jnp.bfloat16)
        for k in range(count):
            one_ref[i + k] = total[k * pairs : (k + 1) * pairs]

    def mid_two(i, count, good):
        even = [cat2e[pl.ds((i + d) * mid1, count * mid1), :] for d in range(2)]
        odd = cat2o[pl.ds(i * mid1, count * mid1), :]
        total = conv([even[0], odd, even[1]], t2a, bias2a)
        for k in range(count):
            row = masked(total[k * mid1 : (k + 1) * mid1], good)
            stage[k % ways, 8 : 8 + mid1, :] = row
            down = stage[k % ways, 15 : 15 + cols2, :]
            up = stage[k % ways, 17 : 17 + cols2, :]
            cat_row = jnp.concatenate([down, row[8 : 8 + cols2], up], axis=1)
            cat2b[at(i + k, cols2), :] = cat_row.astype(jnp.bfloat16)

    def out_two(i, count):
        lhs = [cat2b[pl.ds((i + u) * cols2, count * cols2), :] for u in range(3)]
        total = conv(lhs, t2b, bias2b).astype(jnp.bfloat16)
        for k in range(count):
            two_ref[i + k] = total[k * cols2 : (k + 1) * cols2]

    def mid_three(i, count, good):
        even = [cat3e[pl.ds((i + d) * mid3, count * mid3), :] for d in range(2)]
        odd = cat3o[pl.ds(i * mid3, count * mid3), :]
        total = conv([even[0], odd, even[1]], t3a, bias3a)
        for k in range(count):
            row = masked(total[k * mid3 : (k + 1) * mid3], good)
            stage4[k % ways, 8 : 8 + mid3, :] = row
            down = stage4[k % ways, 15 : 15 + cols3, :]
            up = stage4[k % ways, 17 : 17 + cols3, :]
            cat_row = jnp.concatenate([down, row[8 : 8 + cols3], up], axis=1)
            cat3b[at(i + k, cols3), :] = cat_row.astype(jnp.bfloat16)

    up = near_ref.shape[1]
    cols = 2 * pairs

    def put_out(which):
        return pltpu.make_async_copy(
            result.at[which], out_ref.at[pl.ds(which * up, up)], out_sem.at[which]
        )

    def put(row, value, bias):
        put_row(gather, rows1, row, value, bias)

    def finish(which):
        take_rows(gather, rows1, result.at[which])
        put_out(which).start()

    def bias_tile(at_row):
        return jnp.broadcast_to(bias_ref[at_row : at_row + 1, :], (TILE, up)).T

    def near_lift():
        loads[8].wait()
        near = near_ref[...].astype(jnp.float32)
        near = jnp.concatenate([near, near], axis=0).T.astype(jnp.bfloat16)
        bias = bias_tile(8)
        for r in range(rows1):
            row = one_ref[r].astype(jnp.float32)
            way = r % 2
            expand1[way, pl.ds(0, pairs, stride=2), :] = jnp.where(half_own, row, 0.0)
            expand1[way, pl.ds(1, pairs, stride=2), :] = jnp.where(half_own, 0.0, row)
            put(r, product(near, expand1[way].astype(jnp.bfloat16)), bias)
        finish(0)

    def mid_lift():
        loads[9].wait()
        expand2[...] = jnp.zeros_like(expand2)
        bias = bias_tile(9)
        factor = mid_ref.shape[0]
        weight = stacked(mid_ref)
        for i in range(rows2):
            row = two_ref[i].astype(jnp.float32)
            way = i % 2
            for e in range(factor):
                expand2[way, e, pl.ds(e, cols2, stride=factor), :] = row
            wide_row = jnp.concatenate([expand2[way, e] for e in range(factor)], axis=1)
            total = product(weight, wide_row.astype(jnp.bfloat16))
            for a in range(factor):
                put(i * factor + a, total[a * up : (a + 1) * up], bias)
        finish(1)

    zero.wait_recv(beside)

    def inner_fill(g, carry):
        for k in range(4):
            r = g * 4 + k
            fill1a(r + 2, bev_ref[r], k)
        return carry

    lax.fori_loop(0, rows1 // 4, inner_fill, 0)

    def inner_mid(g, carry):
        mid_one(2 + g * 2, 2, True)
        return carry

    lax.fori_loop(0, (rows1 - 2) // 2, inner_mid, 0)

    def inner_out(g, carry):
        out_one(2 + g * 2, 2)
        return carry

    lax.fori_loop(0, (rows1 - 4) // 2, inner_out, 0)
    zero.wait_recv(across)
    for k in range(2):
        fill1a(k, top0[k], k)
        fill1a(rows1 + 2 + k, bottom0[k], 2 + k)
    mid_one(0, 1, has_up)
    mid_one(1, 1, True)
    mid_one(rows1, 1, True)
    mid_one(rows1 + 1, 1, has_down)
    out_one(0, 2)
    out_one(rows1 - 2, 2)
    one.start(lambda dr, dc: True)

    one.wait_recv(beside)

    def inner_fill2(g, carry):
        for k in range(2):
            r = g * 4 + 2 * k
            fill2a(r + 3, cat2o, one_ref[r], 2 * k)
            fill2a(r + 4, cat2e, one_ref[r + 1], 2 * k + 1)
        return carry

    lax.fori_loop(0, rows1 // 4, inner_fill2, 0)
    for i in range(2, rows2, 2):
        mid_two(i, 2, True)
    mid_two(rows2, 1, True)
    for i in range(2, rows2 - 2, 2):
        out_two(i, 2)
    out_two(rows2 - 2, 1)
    near_lift()
    one.wait_recv(across)
    fill2a(0, cat2e, top1[0], 0)
    fill2a(1, cat2o, top1[1], 1)
    fill2a(2, cat2e, top1[2], 2)
    fill2a(rows1 + 3, cat2o, bottom1[0], 3)
    fill2a(rows1 + 4, cat2e, bottom1[1], 0)
    mid_two(0, 1, has_up)
    mid_two(1, 1, True)
    mid_two(rows2 + 1, 1, has_down)
    out_two(0, 2)
    out_two(rows2 - 1, 1)
    two.start(lambda dr, dc: True)

    two.wait_recv(beside)
    for r in range(rows2):
        fill3a(r + 3, cat3o if r % 2 == 0 else cat3e, two_ref[r], r % ways)
    mid_three(2, rows3 - 1, True)
    mid_lift()
    two.wait_recv(across)
    fill3a(0, cat3e, top2[0], 0)
    fill3a(1, cat3o, top2[1], 1)
    fill3a(2, cat3e, top2[2], 2)
    fill3a(rows2 + 3, cat3o, bottom2[0], 3)
    fill3a(rows2 + 4, cat3e, bottom2[1], 0)
    mid_three(0, 1, has_up)
    mid_three(1, 1, True)
    mid_three(rows3 + 1, 1, has_down)
    lhs = [cat3b[u * cols3 : (u + rows3) * cols3, :] for u in range(3)]
    total = conv(lhs, t3b, bias3b).astype(jnp.bfloat16)
    three_ref[...] = total.reshape(rows3, cols3, chan3)
    three_out = pltpu.make_async_copy(three_ref, three_hbm, load_sem.at[0])
    three_out.start()
    for which in range(2):
        put_out(which).wait()
    three_out.wait()
    for halo in (zero, one, two):
        halo.wait_send()


def levels(bev, convs, lifts, bias):
    rows1, pairs, _ = bev.shape
    w1a, w1b, w2a, w2b, w3a, w3b = convs
    chan1, chan2, chan3 = w1a.shape[2], w2b.shape[2], w3b.shape[2]
    rows2, rows3, cols2, cols3 = rows1 // 2, rows1 // 4, pairs, pairs // 2
    near, mid = lifts
    up, cols = near.shape[1], 2 * pairs
    operands = (bev, *convs, *lifts, bias)
    mid1, mid3 = pairs + 16, cols3 + 16

    def buffers(rows, before, after):
        return [
            pltpu.VMEM((before, pairs, TILE), jnp.bfloat16),
            pltpu.VMEM((after, pairs, TILE), jnp.bfloat16),
            pltpu.VMEM((before + rows + after, SIDE, TILE), jnp.bfloat16),
            pltpu.VMEM((before + rows + after, SIDE, TILE), jnp.bfloat16),
        ]

    def half(*shape):
        return pltpu.VMEM(shape, jnp.bfloat16)

    return pl.pallas_call(
        levels_kernel,
        in_specs=[pl.BlockSpec(memory_space=pl.ANY)] * len(operands),
        out_specs=[pl.BlockSpec(memory_space=pl.ANY)] * 2,
        out_shape=[
            jax.ShapeDtypeStruct((2 * up, rows1, cols), jnp.bfloat16),
            jax.ShapeDtypeStruct((rows3, cols3, chan3), jnp.bfloat16),
        ],
        scratch_shapes=[pltpu.VMEM(operand.shape, operand.dtype) for operand in operands]
        + [
            pltpu.SemaphoreType.DMA((len(operands),)),
            half(rows1, pairs, TILE),
            half(rows2, cols2, chan2),
            half(rows3, cols3, chan3),
        ]
        + buffers(rows1, 2, 2)
        + buffers(rows1, 3, 2)
        + buffers(rows2, 3, 2)
        + [pltpu.SemaphoreType.DMA((3, len(STEPS)))] * 2
        + [
            half(12 * chan1, 2 * chan1),
            half(12 * chan1, 2 * chan1),
            half(12 * chan1, chan2),
            half(9 * chan2, chan2),
            half(9 * chan2, chan3),
            half(9 * chan3, chan3),
            half((rows1 + 4) * mid1, 4 * chan1),
            half((rows1 + 2) * pairs, 4 * chan1),
            half((rows2 + 3) * mid1, 4 * chan1),
            half((rows2 + 2) * mid1, 4 * chan1),
            half((rows2 + 2) * cols2, 3 * chan2),
            half((rows3 + 3) * mid3, 3 * chan2),
            half((rows3 + 2) * mid3, 3 * chan2),
            half((rows3 + 2) * cols3, 3 * chan3),
            pltpu.VMEM((4, mid1 + 16, TILE), jnp.float32),
            pltpu.VMEM((4, cols2 + 2 * SIDE + 16, TILE), jnp.float32),
            pltpu.VMEM((4, mid3 + 16, chan3), jnp.float32),
            half(2, up, rows1, cols),
            pltpu.VMEM((2, cols, TILE), jnp.float32),
            pltpu.VMEM((2, mid.shape[0], cols, TILE), jnp.float32),
            pltpu.VMEM((cols // TILE, up * rows1, TILE), jnp.float32),
            pltpu.SemaphoreType.DMA((2,)),
        ],
        compiler_params=pltpu.CompilerParams(collective_id=8, has_side_effects=True),
        name="levels",
    )(*operands)


def on_device(
    points,
    pillar_cell,
    point_count,
    tile_count,
    point_embed,
    point_mix,
    first_conv,
    second_conv,
    third_conv,
    fourth_conv,
    fifth_conv,
    sixth_conv,
    near_lift,
    mid_lift,
    far_lift,
    biases,
):
    tile_num = tile_count.shape[0]
    capacity = points.shape[2] // tile_num
    bias = biases.reshape(-1, TILE)
    vectors, places = encode_all(
        points,
        point_count.reshape(tile_num, 1, capacity),
        pillar_cell.reshape(tile_num, 1, capacity),
        tile_count,
        jnp.transpose(point_embed),
        point_mix,
        bias,
    )
    chan = point_mix.shape[0]
    bev = scatter_max(places.reshape(-1), vectors)
    bev = bev.reshape(ROWS_DEV, COLS_DEV // 2, 2 * chan)
    convs = (
        first_conv,
        second_conv,
        jnp.transpose(third_conv, (0, 1, 3, 2)),
        fourth_conv,
        fifth_conv,
        sixth_conv,
    )
    near = jnp.transpose(near_lift, (0, 1, 3, 2)).reshape(near_lift.shape[3], near_lift.shape[2])
    upper, three = levels(bev, convs, (near, mid_lift), bias)
    return far_lift_all(upper, three, far_lift, bias)


def solution(mesh):
    return jax.shard_map(
        on_device,
        mesh=mesh,
        in_specs=(
            P(None, None, ("slab", "row", "col")),
            P(("slab", "row", "col")),
            P(("slab", "row", "col")),
            P(("slab", "row", "col")),
            P(),
            P(),
            P(),
            P(),
            P(),
            P(),
            P(),
            P(),
            P(),
            P(),
            P(),
            P(),
        ),
        out_specs=P(None, ("slab", "row"), "col"),
        check_vma=False,
    )
```
